256 devices in a mesh: role: 4 (over y), gx: 16 (over z, core), gz: 4 (over x).
Axes of the slice: x: 4, y: 4, z: 8, core: 2. Of those that a mesh axis runs over, the one named last changes fastest.
Arguments:
- pressure_old: float32 [64, 1024, 512], P('gz', 'gx', 'role'), may hold values from -2.5 to -0.2
- vg_alpha: float32 [64, 1024, 512], P('gz', 'gx', 'role'), may hold values from 0.5 to 1.5
- vg_n: float32 [64, 1024, 512], P('gz', 'gx', 'role'), may hold values from 1.3 to 2.5
- conductivity_sat: float32 [64, 1024, 512], P('gz', 'gx', 'role'), may hold values from 0.05 to 1
- porosity: float32 [64, 1024, 512], P('gz', 'gx', 'role'), may hold values from 0.25 to 0.45
- tile_owner: int32 [1024, 4], replicated, may hold values from -1 to 63, as said below
- land_temp: float32 [4, 64, 48, 16, 128], P('role', ('gx', 'gz')), may hold values from -6 to 6
- transpiration: float32 [4, 64, 48, 128], P('role', ('gx', 'gz')), may hold values from 0.2 to 1
- air_temp: float32 [4, 64, 48, 128], P('role', ('gx', 'gz')), may hold values from -6 to 6
- root_layers: int32 [4, 64, 48, 128], P('role', ('gx', 'gz')), may hold values from 1 to 16
Outputs:
- pressure_new: float32 [64, 1024, 512], P('gz', 'gx', 'role')
- land_temp_new: float32 [4, 64, 48, 16, 128], P('role', ('gx', 'gz'))
The draws below stay inside these ranges and needn't reach their ends.
Inputs may be any that keep to these rules, and one draw needn't show every extreme that they name: `tile_owner`: -1 marks an inactive tile; otherwise the value is the land device, numbered along gx and gz with gz fastest, within the tile's role group; at most 3 tiles of one block have the same owner, and in every block one owner holds exactly 3 of them.
All inputs are finite; a program needn't handle non-finite values.
Results may differ from the reference program's by a relative error of at most 0.00002.
Values sent between devices are 32-bit elements; how exact they have to be, the bound alone decides.
A program may use at most 64 MiB of HBM per device.

```python
import math
import jax
import jax.numpy as jnp
from jax import lax

LAYERS = 16
LEVELS_PER_LAYER = 4
NZ = 64
CX = 64
CY = 128
CAP = 3
SWEEPS = 3
HEAT_STEPS = 4
NX = 1024
NY = 512
GROUPS = 64
SLOTS = 48
N_ROLE = 4
N_GX = 16
N_GZ = 4


def draw_tile_owner(key, part):
    groups = N_GX * N_GZ
    blocks = N_GX * N_ROLE
    key_heavy, key_perm, key_rot, key_coin = jax.random.split(key, 4)
    heavy = jax.random.randint(key_heavy, (N_ROLE,), 0, groups)
    perm_keys = jax.random.split(key_perm, blocks)
    position = jax.vmap(lambda single: jax.random.permutation(single, CX))(perm_keys)
    rotation = jax.random.randint(key_rot, (blocks, 1), 0, groups - 1)
    coins = jax.random.randint(key_coin, (blocks, CX), 0, 4) < 3
    heavy_block = jnp.tile(heavy, N_GX)[:, None]
    later = position - CAP
    others = (later + rotation) % (groups - 1)
    other_owner = others + (others >= heavy_block).astype(jnp.int32)
    active_other = (later >= 0) & (later < (groups - 1) * CAP) & coins
    owner = jnp.where(position < CAP, heavy_block, jnp.where(active_other, other_owner, -1))
    owner = owner.astype(jnp.int32).reshape(N_GX, N_ROLE, CX).transpose(0, 2, 1)
    return owner.reshape(N_GX * CX, N_ROLE)


def place_ends(drawn, key, smallest, high):
    extent = drawn.shape
    index_at = [jax.random.randint(jax.random.fold_in(key, axis), (), 0, extent[axis]) for axis in range(len(extent))]
    drawn = drawn.at[tuple(index_at)].set(smallest)
    longest = extent.index(max(extent))
    index_at[longest] = (index_at[longest] + 1) % extent[longest]
    return drawn.at[tuple(index_at)].set(high)


def block_levels(key, extent, cuts, smallest, largest):
    def one(dim, blocks):
        draws = jax.random.uniform(jax.random.fold_in(jax.random.fold_in(key, 6), dim), (blocks,), jnp.float32, smallest / len(cuts), largest / len(cuts))
        return jnp.repeat(jnp.exp(draws), extent[dim] // blocks).reshape((-1,) + (1,) * (len(extent) - dim - 1))

    gain = one(*cuts[0])
    for cut in cuts[1:]:
        gain = gain * one(*cut)
    return gain


def gaussian(stream_key, extent, scale, limit, cuts=(), held_as=jnp.bfloat16):
    array = jax.random.normal(stream_key, extent, jnp.float32) * scale
    if len(cuts) > 0:
        array = block_levels(stream_key, extent, cuts, -0.22, 0.18) * array
    return jnp.clip(array, min=-limit, max=limit).astype(held_as)


def setup_inputs(seed: int = 0) -> dict:
    arg_keys = jax.random.split(jax.random.key(seed), 11)
    return {
        "pressure_old": jnp.clip(-2.5 + 2.3 * jax.random.uniform(arg_keys[0], (NZ, NX, NY), jnp.float32) ** block_levels(arg_keys[0], (NZ, NX, NY), ((0, 4), (1, 16), (2, 4)), -0.2, 0.2), -2.5, -0.2),
        "vg_alpha": jnp.clip(jnp.exp(math.log(1.5) - 1.0986123 * jax.random.uniform(arg_keys[1], (NZ, NX, NY), jnp.float32) ** block_levels(arg_keys[1], (NZ, NX, NY), ((0, 4), (1, 16), (2, 4)), -0.2, 0.2)), 0.5, 1.5),
        "vg_n": jnp.clip(1.3 + 1.2 * jax.random.uniform(arg_keys[2], (NZ, NX, NY), jnp.float32) ** block_levels(arg_keys[2], (NZ, NX, NY), ((0, 4), (1, 16), (2, 4)), -0.2, 0.2), 1.3, 2.5),
        "conductivity_sat": jnp.clip(jnp.exp(math.log(1.0) - 2.9957323 * jax.random.uniform(arg_keys[3], (NZ, NX, NY), jnp.float32) ** block_levels(arg_keys[3], (NZ, NX, NY), ((0, 4), (1, 16), (2, 4)), -0.2, 0.2)), 0.05, 1.0),
        "porosity": jnp.clip(0.25 + 0.19999999 * jax.random.uniform(arg_keys[4], (NZ, NX, NY), jnp.float32) ** block_levels(arg_keys[4], (NZ, NX, NY), ((0, 4), (1, 16), (2, 4)), -0.2, 0.2), 0.25, 0.45),
        "tile_owner": draw_tile_owner(jax.random.fold_in(arg_keys[10], 71), 0),
        "land_temp": gaussian(arg_keys[6], (N_ROLE, GROUPS, SLOTS, LAYERS, CY), 1.0, 6.0, ((0, 4), (1, 64)), jnp.float32),
        "transpiration": jnp.clip(0.2 + 0.8 * jax.random.uniform(arg_keys[7], (N_ROLE, GROUPS, SLOTS, CY), jnp.float32) ** block_levels(arg_keys[7], (N_ROLE, GROUPS, SLOTS, CY), ((0, 4), (1, 64)), -0.2, 0.2), 0.2, 1.0),
        "air_temp": gaussian(arg_keys[8], (N_ROLE, GROUPS, SLOTS, CY), 1.5, 6.0, ((0, 4), (1, 64)), jnp.float32),
        "root_layers": place_ends(jax.random.randint(arg_keys[9], (N_ROLE, GROUPS, SLOTS, CY), 1, 17), jax.random.fold_in(arg_keys[9], 1), 1, 16).astype(jnp.int32),
    }


def soil_curves(head, alpha, vgn, ksat):
    suction = jnp.sqrt(head * head + 0.01)
    logx = vgn * jnp.log(alpha * suction)
    expo = 1.0 - 1.0 / vgn
    softer = jnp.log1p(jnp.exp(logx))
    satur = jnp.exp(-expo * softer)
    cond = ksat * jnp.sqrt(satur) * (1.0 - jnp.exp(expo * (logx - softer))) ** 2
    return (satur, cond)

def layer_mean(values, axis):
    shape = values.shape
    split = shape[:axis] + (shape[axis] // 4, 4) + shape[axis + 1:]
    parts = values.reshape(split)
    first = lax.index_in_dim(parts, 0, axis + 1, keepdims=False)
    second = lax.index_in_dim(parts, 1, axis + 1, keepdims=False)
    third = lax.index_in_dim(parts, 2, axis + 1, keepdims=False)
    fourth = lax.index_in_dim(parts, 3, axis + 1, keepdims=False)
    return (first + second + third + fourth) * 0.25

def land_step(satur, head, temps, tpot, air, roots):
    nlayer = satur.shape[-2]
    layer = jnp.arange(nlayer, dtype=jnp.float32)[:, None]
    depth = jnp.arange(nlayer, dtype=jnp.int32)[:, None]
    weights = jnp.exp(-layer / 4.0) * (depth < roots[..., None, :]).astype(jnp.float32)
    weights = weights / lax.optimization_barrier(jnp.sum(weights, axis=-2, keepdims=True))
    stress = 1.0 / (1.0 + head * head / 2.25)
    uptake = tpot[..., None, :] * weights * stress
    kappa = 0.25 + 0.9 * satur
    inner = 0.5 * (kappa[..., :-1, :] + kappa[..., 1:, :])
    k_above = jnp.concatenate([kappa[..., :1, :], inner], axis=-2)
    k_below = jnp.concatenate([inner, jnp.zeros_like(kappa[..., :1, :])], axis=-2)
    for substep in range(HEAT_STEPS):
        above = jnp.concatenate([air[..., None, :], temps[..., :-1, :]], axis=-2)
        below = jnp.concatenate([temps[..., 1:, :], temps[..., -1:, :]], axis=-2)
        temps = temps + 0.2 * (k_above * (above - temps) + k_below * (below - temps)) - 0.3 * uptake
    return (uptake, temps)

def sweep_update(padh, padk, masks, head, cond, water, theta_old, sink, omega):
    mask_up, mask_down, mask_xm, mask_xp, mask_ym, mask_yp = masks
    near_up = padh[:-2, 1:-1, 1:-1]
    near_down = padh[2:, 1:-1, 1:-1]
    near_xm = padh[1:-1, :-2, 1:-1]
    near_xp = padh[1:-1, 2:, 1:-1]
    near_ym = padh[1:-1, 1:-1, :-2]
    near_yp = padh[1:-1, 1:-1, 2:]
    kf_up = 0.5 * (cond + padk[:-2, 1:-1, 1:-1]) * mask_up
    kf_down = 0.5 * (cond + padk[2:, 1:-1, 1:-1]) * mask_down
    kf_xm = 0.5 * (cond + padk[1:-1, :-2, 1:-1]) * mask_xm
    kf_xp = 0.5 * (cond + padk[1:-1, 2:, 1:-1]) * mask_xp
    kf_ym = 0.5 * (cond + padk[1:-1, 1:-1, :-2]) * mask_ym
    kf_yp = 0.5 * (cond + padk[1:-1, 1:-1, 2:]) * mask_yp
    flux = kf_up * (head - near_up) + kf_down * (head - near_down)
    flux = flux + kf_xm * (head - near_xm) + kf_xp * (head - near_xp)
    flux = flux + kf_ym * (head - near_ym) + kf_yp * (head - near_yp)
    resid = water - theta_old + flux + (kf_down - kf_up) + sink
    diag = 1.0 + (kf_up + kf_down + kf_xm + kf_xp + kf_ym + kf_yp)
    return head - omega * resid / diag

def reference(pressure_old, vg_alpha, vg_n, conductivity_sat, porosity, tile_owner, land_temp, transpiration, air_temp, root_layers):
    groups = N_GX * N_GZ
    satur_old, cond_old = soil_curves(pressure_old, vg_alpha, vg_n, conductivity_sat)
    theta_old = porosity * satur_old
    layer_sat = layer_mean(satur_old, 0)
    layer_head = layer_mean(pressure_old, 0)
    tile_sat = layer_sat.reshape(LAYERS, NX, N_ROLE, CY).transpose(1, 2, 0, 3)
    tile_head = layer_head.reshape(LAYERS, NX, N_ROLE, CY).transpose(1, 2, 0, 3)
    owners3 = tile_owner.reshape(N_GX, CX, N_ROLE)
    onehot = (owners3[..., None] == jnp.arange(groups, dtype=jnp.int32)).astype(jnp.int32)
    before = (jnp.cumsum(onehot, axis=1) - onehot).astype(jnp.int32)
    rank = lax.optimization_barrier(jnp.sum(before * onehot, axis=-1)).astype(jnp.int32).reshape(NX, N_ROLE)
    block_row = (jnp.arange(NX, dtype=jnp.int32) // CX)[:, None]
    slot = jnp.broadcast_to(block_row * CAP + rank, (NX, N_ROLE)).astype(jnp.int32)
    active = tile_owner >= 0
    owner_safe = jnp.where(active, tile_owner, 0).astype(jnp.int32)
    owner_drop = jnp.where(active, tile_owner, groups).astype(jnp.int32)
    role_index = jnp.broadcast_to(jnp.arange(N_ROLE, dtype=jnp.int32)[None, :], (NX, N_ROLE))
    temps = land_temp[role_index, owner_safe, slot]
    tpot = transpiration[role_index, owner_safe, slot]
    air = air_temp[role_index, owner_safe, slot]
    roots = root_layers[role_index, owner_safe, slot]
    uptake, new_temps = land_step(tile_sat, tile_head, temps, tpot, air, roots)
    land_temp_new = land_temp.at[role_index, owner_drop, slot].set(new_temps, mode='drop')
    uptake = uptake * active.astype(jnp.float32)[:, :, None, None]
    sink = uptake.transpose(2, 0, 1, 3).reshape(LAYERS, NX, NY)
    sink = jnp.repeat(sink, LEVELS_PER_LAYER, axis=0)
    zglob = jnp.arange(NZ)
    xglob = jnp.arange(NX)
    yglob = jnp.arange(NY)
    masks = ((zglob > 0).astype(jnp.float32)[:, None, None], (zglob < NZ - 1).astype(jnp.float32)[:, None, None], (xglob > 0).astype(jnp.float32)[None, :, None], (xglob < NX - 1).astype(jnp.float32)[None, :, None], (yglob > 0).astype(jnp.float32)[None, None, :], (yglob < NY - 1).astype(jnp.float32)[None, None, :])
    head = pressure_old
    cond = cond_old
    water = theta_old
    for sweep_index in range(SWEEPS):
        if sweep_index > 0:
            satur, cond = soil_curves(head, vg_alpha, vg_n, conductivity_sat)
            water = porosity * satur
        omega = 1.0 / (1.0 + 0.6 * math.cos(math.pi * (2 * sweep_index + 1) / (2 * SWEEPS)))
        head = sweep_update(jnp.pad(head, 1), jnp.pad(cond, 1), masks, head, cond, water, theta_old, sink, omega)
    return (head, land_temp_new)
```

```python
import functools
import math

import jax
import jax.numpy as jnp
from jax import lax
from jax.experimental import pallas as pl
from jax.experimental.pallas import tpu as pltpu
from jax.sharding import PartitionSpec as P

LEVELS_PER_LAYER = 4
CAP = 3
SWEEPS = 3
HEAT_STEPS = 4
LOG2E = 1.0 / math.log(2.0)
CHUNK = 32
PAD = 8
MESH = pl.DeviceIdType.MESH
OMEGAS = [
    1.0 / (1.0 + 0.6 * math.cos(math.pi * (2 * k + 1) / (2 * SWEEPS))) for k in range(SWEEPS)
]


def curves(head, c1, c0, m, ks):
    lx = c1 * jnp.log(head * head + 0.01) + c0
    soft = jnp.log(1.0 + jnp.exp2(lx)) * LOG2E
    root = jnp.exp2(-0.5 * (m * soft))
    gap = 1.0 - jnp.exp2(m * (lx - soft))
    return root * root, ks * root * (gap * gap)


def split3(x):
    hi = x.astype(jnp.bfloat16)
    rest = x - hi.astype(jnp.float32)
    mid = rest.astype(jnp.bfloat16)
    return hi, mid, (rest - mid.astype(jnp.float32)).astype(jnp.bfloat16)


def kernel(
    n_role,
    n_gx,
    n_gz,
    p_hbm,
    al_hbm,
    vn_hbm,
    ks_hbm,
    po_hbm,
    own_hbm,
    lt_hbm,
    tr_hbm,
    ai_hbm,
    ro_hbm,
    out_p,
    out_lt,
    p_v,
    c0_v,
    c1_v,
    ks_v,
    po_v,
    m_v,
    th_v,
    ra_v,
    da_v,
    hp,
    kp,
    xs,
    xh,
    ys,
    yh,
    own_v,
    lt_v,
    tr_v,
    ai_v,
    ro_v,
    sel_v,
    get_v,
    act_v,
    cnt_v,
    tp_v,
    rt_v,
    tq_v,
    rq_v,
    sk_v,
    lh_v,
    mean_v,
    tx_v,
    rx_v,
    load_sem,
    zt_send,
    zt_recv,
    xt_send,
    xt_recv,
    h_send,
    h_recv,
    land_send,
    land_recv,
    line_sem,
):
    levels, rows, cols = p_hbm.shape
    layers = levels // LEVELS_PER_LAYER
    groups = n_gx * n_gz
    tile = 2 * layers
    per = CAP * tile
    role = lax.axis_index("role")
    gx = lax.axis_index("gx")
    gz = lax.axis_index("gz")
    me = gx * n_gz + gz

    barrier = pltpu.get_barrier_semaphore()

    def greet_gx(i, c):
        pl.semaphore_signal(
            barrier, inc=1, device_id={"gx": lax.rem(gx + i, n_gx)}, device_id_type=MESH
        )
        return c

    def greet_gz(i, c):
        pl.semaphore_signal(
            barrier, inc=1, device_id={"gz": lax.rem(gz + i, n_gz)}, device_id_type=MESH
        )
        return c

    lax.fori_loop(1, n_gx, greet_gx, 0)
    lax.fori_loop(1, n_gz, greet_gz, 0)
    for step in (1, n_role - 1):
        pl.semaphore_signal(
            barrier, inc=1, device_id={"role": lax.rem(role + step, n_role)}, device_id_type=MESH
        )

    pairs = (
        (tr_hbm, tr_v),
        (ro_hbm, ro_v),
        (own_hbm, own_v),
        (p_hbm, p_v),
        (al_hbm, c0_v),
        (vn_hbm, c1_v),
        (ks_hbm, ks_v),
        (po_hbm, po_v),
        (lt_hbm, lt_v),
        (ai_hbm, ai_v),
    )
    loads = [pltpu.make_async_copy(a, b, load_sem.at[i]) for i, (a, b) in enumerate(pairs)]
    for load in loads:
        load.start()

    loads[0].wait()
    loads[1].wait()
    for b in range(n_gx):
        tp_v[b, CAP:4, :] = jnp.zeros((1, cols), jnp.float32)
        tp_v[b, 4 + CAP :, :] = jnp.zeros((1, cols), jnp.float32)
        tp_v[b, 0:CAP, :] = tr_v[b * CAP : (b + 1) * CAP, :]
        tp_v[b, 4 : 4 + CAP, :] = ro_v[b * CAP : (b + 1) * CAP, :].astype(jnp.float32)

    loads[2].wait()
    lane1 = lax.broadcasted_iota(jnp.int32, (1, 128), 1)
    sub4 = lax.broadcasted_iota(jnp.int32, (n_role, 128), 0)

    def role_lanes(start):
        return jnp.sum(
            jnp.where(sub4 == role, own_v[:, pl.ds(start, 128)], 0), axis=0, keepdims=True
        )

    pair = role_lanes(pl.multiple_of((gx // 2) * 128, 128))
    own = jnp.where(lax.rem(gx, 2) == 1, pltpu.roll(pair, 64, 1), pair)
    ii = lax.broadcasted_iota(jnp.int32, (128, 128), 0)
    jj = lax.broadcasted_iota(jnp.int32, (128, 128), 1)
    by_lane = jnp.broadcast_to(own, (128, 128))
    by_sub = jnp.transpose(by_lane)
    earlier = (by_lane == by_sub) & (ii < jj) & (ii < rows)
    rank_lane = jnp.sum(jnp.where(earlier, 1, 0), axis=0, keepdims=True)
    rank_sub = jnp.transpose(jnp.broadcast_to(rank_lane, (128, 128)))
    key = jnp.where((own >= 0) & (lane1 < rows), own * CAP + rank_lane + 1, 0)
    key = jnp.broadcast_to(key + pltpu.roll(key, 64, 1), (groups * CAP, 128))
    slot = lax.broadcasted_iota(jnp.int32, (groups * CAP, 128), 0) + 1
    wide = lax.broadcasted_iota(jnp.int32, (groups * CAP, 128), 1)
    pick = key == slot
    sel_v[:, 0:128] = jnp.where(pick, 1.0, 0.0).astype(jnp.bfloat16)
    sel_v[:, 128:256] = jnp.where(pick & (wide < rows), 1.0, 0.0).astype(jnp.bfloat16)
    at = jnp.where(by_sub >= 0, by_sub * 8 + rank_sub, -8)[:rows]
    for t in range(groups * 8 // 128):
        for f in range(2):
            hit = at + 4 * f == jj[:rows] + t * 128
            get_v[f * rows : (f + 1) * rows, t * 128 : (t + 1) * 128] = jnp.where(
                hit, 1.0, 0.0
            ).astype(jnp.bfloat16)
    act_v[...] = jnp.where(by_sub[:rows] >= 0, 1.0, 0.0)
    for t in range(n_gx // 2):
        hit = jnp.where(role_lanes(t * 128) == me, 1.0, 0.0)
        for side in range(2):
            part = jnp.where((lane1 < 64) == (side == 0), hit, 0.0)
            cnt_v[2 * t + side : 2 * t + side + 1, :] = jnp.broadcast_to(
                jnp.sum(part, axis=1, keepdims=True), (1, 128)
            )

    lane = lax.broadcasted_iota(jnp.int32, (CHUNK, 128), 1)

    def pack_y(k, d, r0, level, head, cond):
        at0 = level - 1
        edge = 0 if d == 0 else 127
        h = pltpu.roll(head, at0 + (128 - edge if edge else 0), 1)
        c = pltpu.roll(cond, at0 + levels + (128 - edge if edge else 0), 1)
        old = ys[k, d, pl.ds(r0, CHUNK), :]
        ys[k, d, pl.ds(r0, CHUNK), :] = jnp.where(
            lane == at0, h, jnp.where(lane == at0 + levels, c, old)
        )

    def put(k, level, r0, head, cond):
        hp[k, level, pl.ds(PAD + r0, CHUNK), :] = head
        kp[k, level, pl.ds(PAD + r0, CHUNK), :] = cond
        at0 = level - 1
        if r0 == 0:
            xs[k, 0, 0, pl.ds(at0, 1), :] = head[0:1]
            xs[k, 0, 1, pl.ds(at0, 1), :] = cond[0:1]
        if r0 + CHUNK == rows:
            xs[k, 1, 0, pl.ds(at0, 1), :] = head[CHUNK - 1 :]
            xs[k, 1, 1, pl.ds(at0, 1), :] = cond[CHUNK - 1 :]
        for d in range(2):
            pack_y(k, d, r0, level, head, cond)

    def remote(src, dst, k, slot, dst_slot, where):
        return pltpu.make_async_remote_copy(
            src_ref=src,
            dst_ref=dst,
            send_sem=h_send.at[k * 8 + slot],
            recv_sem=h_recv.at[k * 8 + dst_slot],
            device_id=where,
            device_id_type=MESH,
        )

    def faces_z(k):
        made = []
        for d in range(2):
            to = lax.rem(gz + (n_gz - 1 if d == 0 else 1), n_gz)
            for f, ref in enumerate((hp, kp)):
                src = ref.at[k, 1 if d == 0 else levels, pl.ds(PAD, rows), :]
                dst = ref.at[k, levels + 1 if d == 0 else 0, pl.ds(PAD, rows), :]
                made.append(remote(src, dst, k, 4 + 2 * f + d, 4 + 2 * f + 1 - d, {"gz": to}))
        return made

    def faces_xy(k):
        made = []
        for d in range(2):
            to = lax.rem(gx + (n_gx - 1 if d == 0 else 1), n_gx)
            made.append(remote(xs.at[k, d], xh.at[k, 1 - d], k, d, 1 - d, {"gx": to}))
        for d in range(2):
            to = lax.rem(role + (n_role - 1 if d == 0 else 1), n_role)
            made.append(remote(ys.at[k, d], yh.at[k, 1 - d], k, 2 + d, 2 + 1 - d, {"role": to}))
        return made

    mean_v[:, CAP * rows :, :] = jnp.zeros((layers, 256 - CAP * rows, 2 * cols), jnp.bfloat16)
    for load in loads[3:8]:
        load.wait()

    def start_layer(j, c):
        for r0 in range(0, rows, CHUNK):
            rs = pl.ds(r0, CHUNK)
            sum_s = None
            sum_h = None
            for i in range(LEVELS_PER_LAYER):
                z = j * LEVELS_PER_LAYER + i
                head = p_v[z, rs, :]
                vn = c1_v[z, rs, :]
                c0 = vn * jnp.log(c0_v[z, rs, :]) * LOG2E
                c1 = (0.5 * LOG2E) * vn
                m = 1.0 - 1.0 / vn
                ks = 0.5 * ks_v[z, rs, :]
                c0_v[z, rs, :] = c0
                c1_v[z, rs, :] = c1
                m_v[z, rs, :] = m
                ks_v[z, rs, :] = ks
                sat, cond = curves(head, c1, c0, m, ks)
                th_v[z, rs, :] = po_v[z, rs, :] * sat
                put(0, z + 1, r0, head, cond)
                sum_s = sat if sum_s is None else sum_s + sat
                sum_h = head if sum_h is None else sum_h + head
            mean_h = sum_h * 0.25
            lh_v[j, rs, :] = mean_h
            for f, mean in enumerate((mean_h, sum_s * 0.25)):
                for part, value in enumerate(split3(mean)):
                    mean_v[j, part * rows + r0 : part * rows + r0 + CHUNK, f * cols : (f + 1) * cols] = value
        return c

    started = []
    lax.fori_loop(0, 2, lambda i, c: start_layer(i * (layers - 1), c), 0)

    pl.semaphore_wait(barrier, (n_gx - 1) + (n_gz - 1) + 2)

    def tell_line(i, c):
        pl.semaphore_signal(
            line_sem, inc=1, device_id={"gz": lax.rem(gz + i, n_gz)}, device_id_type=MESH
        )
        return c

    lax.fori_loop(1, n_gz, tell_line, 0)

    def zt_copy(i):
        to = lax.rem(gx + i, n_gx)
        return pltpu.make_async_remote_copy(
            src_ref=tp_v.at[to],
            dst_ref=rt_v.at[gx, gz],
            send_sem=zt_send,
            recv_sem=zt_recv,
            device_id={"gx": to},
            device_id_type=MESH,
        )

    def zt_start(i, c):
        zt_copy(i).start()
        return c

    lax.fori_loop(1, n_gx, zt_start, 0)
    rt_v[gx, gz] = tp_v[gx]

    for copy in faces_z(0):
        copy.start()
        started.append(copy)
    lax.fori_loop(1, layers - 1, start_layer, 0)
    for copy in faces_xy(0):
        copy.start()
        started.append(copy)

    for j in range(layers):
        out = jnp.dot(sel_v[...], mean_v[j], preferred_element_type=jnp.float32)
        tx_v[pl.ds(j, groups * CAP, stride=tile), :] = out[:, :cols]
        tx_v[pl.ds(layers + j, groups * CAP, stride=tile), :] = out[:, cols:]
    rx_v[pl.ds(pl.multiple_of(me * per, 8), per), :] = tx_v[
        pl.ds(pl.multiple_of(me * per, 8), per), :
    ]
    pl.semaphore_wait(line_sem, n_gz - 1)

    def land_start(i, c):
        to_gx = lax.rem(gx + i // n_gz, n_gx)
        to_gz = lax.rem(gz + lax.rem(i, n_gz), n_gz)
        to = to_gx * n_gz + to_gz
        pltpu.make_async_remote_copy(
            src_ref=tx_v.at[pl.ds(pl.multiple_of(to * per, 8), per), :],
            dst_ref=rx_v.at[pl.ds(pl.multiple_of(me * per, 8), per), :],
            send_sem=land_send,
            recv_sem=land_recv,
            device_id={"gx": to_gx, "gz": to_gz},
            device_id_type=MESH,
        ).start()
        return c

    cut1 = groups // 4
    cut2 = groups // 2
    lax.fori_loop(1, cut1, land_start, 0)

    def drain(ref, count, sem):
        pltpu.make_async_copy(ref.at[pl.ds(0, count)], ref.at[pl.ds(0, count)], sem).wait()

    drain(tp_v, n_gx - 1, zt_recv)

    def xt_copy(i):
        return pltpu.make_async_remote_copy(
            src_ref=rt_v.at[:, gz],
            dst_ref=rt_v.at[:, gz],
            send_sem=xt_send,
            recv_sem=xt_recv,
            device_id={"gz": lax.rem(gz + i, n_gz)},
            device_id_type=MESH,
        )

    for i in range(1, n_gz):
        xt_copy(i).start()

    at_lo = role > 0
    at_hi = role < n_role - 1

    def wait_faces(k):
        for slot, ref in ((0, xh.at[k, 0]), (1, xh.at[k, 1]), (2, yh.at[k, 0]), (3, yh.at[k, 1])):
            pltpu.make_async_copy(ref, ref, h_recv.at[k * 8 + slot]).wait()
        for f, ref in enumerate((hp, kp)):
            for d in range(2):
                view = ref.at[k, 0 if d == 0 else levels + 1, pl.ds(PAD, rows), :]
                pltpu.make_async_copy(view, view, h_recv.at[k * 8 + 4 + 2 * f + d]).wait()

        @pl.when(gz == 0)
        def _():
            hp[k, 0, pl.ds(PAD, rows), :] = hp[k, 1, pl.ds(PAD, rows), :]
            kp[k, 0, pl.ds(PAD, rows), :] = -kp[k, 1, pl.ds(PAD, rows), :]

        @pl.when(gz == n_gz - 1)
        def _():
            hp[k, levels + 1, pl.ds(PAD, rows), :] = hp[k, levels, pl.ds(PAD, rows), :]
            kp[k, levels + 1, pl.ds(PAD, rows), :] = -kp[k, levels, pl.ds(PAD, rows), :]

    def put_rows(k, level):
        at0 = pl.ds(level - 1, 1)
        for d, row, edge, inside in ((0, PAD - 1, PAD, gx > 0), (1, PAD + rows, PAD + rows - 1, gx < n_gx - 1)):
            hp[k, level, row : row + 1, :] = jnp.where(
                inside, xh[k, d, 0, at0, :], hp[k, level, edge : edge + 1, :]
            )
            kp[k, level, row : row + 1, :] = jnp.where(
                inside, xh[k, d, 1, at0, :], -kp[k, level, edge : edge + 1, :]
            )

    def stencil(k, level, r0):
        def cut(ref, z, shift):
            return ref[k, z, pl.ds(PAD + r0 + shift, CHUNK), :]

        h, c = cut(hp, level, 0), cut(kp, level, 0)
        kf_up = c + cut(kp, level - 1, 0)
        kf_dn = c + cut(kp, level + 1, 0)
        kf_xm = c + cut(kp, level, -1)
        kf_xp = c + cut(kp, level, 1)
        at0 = level - 1
        side0 = yh[k, 0, pl.ds(r0, CHUNK), :]
        side1 = yh[k, 1, pl.ds(r0, CHUNK), :]
        first, last = lane == 0, lane == 127
        h_ym = jnp.where(
            first, jnp.where(at_lo, pltpu.roll(side0, 128 - at0, 1), h), pltpu.roll(h, 1, 1)
        )
        c_ym = jnp.where(
            first,
            jnp.where(at_lo, pltpu.roll(side0, 128 - levels - at0, 1), -c),
            pltpu.roll(c, 1, 1),
        )
        h_yp = jnp.where(
            last, jnp.where(at_hi, pltpu.roll(side1, 127 - at0, 1), h), pltpu.roll(h, 127, 1)
        )
        c_yp = jnp.where(
            last,
            jnp.where(at_hi, pltpu.roll(side1, 127 - levels - at0, 1), -c),
            pltpu.roll(c, 127, 1),
        )
        kf_ym = c + c_ym
        kf_yp = c + c_yp
        flux = kf_up * (h - cut(hp, level - 1, 0)) + kf_dn * (h - cut(hp, level + 1, 0))
        flux = flux + kf_xm * (h - cut(hp, level, -1)) + kf_xp * (h - cut(hp, level, 1))
        flux = flux + kf_ym * (h - h_ym) + kf_yp * (h - h_yp)
        diag = 1.0 + ((kf_up + kf_dn) + (kf_xm + kf_xp) + (kf_ym + kf_yp))
        return h, flux + (kf_dn - kf_up), diag

    wait_faces(0)

    def first_half(z, c):
        level = z + 1
        put_rows(0, level)
        for r0 in range(0, rows, CHUNK):
            _, resid, diag = stencil(0, level, r0)
            ra_v[z, pl.ds(r0, CHUNK), :] = resid
            da_v[z, pl.ds(r0, CHUNK), :] = OMEGAS[0] / diag
        return c

    lax.fori_loop(0, levels, first_half, 0)
    lax.fori_loop(cut1, cut2, land_start, 0)

    ref3 = rt_v.at[:, pl.ds(0, n_gz - 1)]
    pltpu.make_async_copy(ref3, ref3, xt_recv).wait()

    pieces = jnp.concatenate(split3(rt_v[...].reshape(groups * 8, cols)), axis=1)
    got = jnp.dot(get_v[...], pieces, preferred_element_type=jnp.float32)
    got = got[:, :cols] + got[:, cols : 2 * cols] + got[:, 2 * cols :]
    tq_v[...] = got[:rows]
    rq_v[...] = got[rows:] + (1.0 - act_v[...])

    def root_weight(depth, roots):
        return jnp.where(depth < roots, math.exp(-depth / 4.0), 0.0)

    for r0 in range(0, rows, CHUNK):
        rs = pl.ds(r0, CHUNK)
        roots = rq_v[rs, :]
        total = root_weight(0, roots)
        for depth in range(1, layers * n_gz):
            total = total + root_weight(depth, roots)
        scale = tq_v[rs, :]
        for j in range(layers):
            depth = (gz * layers + j).astype(jnp.float32)
            weight = jnp.where(
                depth < roots, jnp.exp(jnp.full((CHUNK, 128), -0.25, jnp.float32) * depth), 0.0
            )
            lh = lh_v[j, rs, :]
            stress = 1.0 / (1.0 + lh * lh * (1.0 / 2.25))
            sk_v[j, rs, :] = scale * (weight / total) * stress

    def curve_into(k, z, r0, head):
        rs = pl.ds(r0, CHUNK)
        sat, cond = curves(head, c1_v[z, rs, :], c0_v[z, rs, :], m_v[z, rs, :], ks_v[z, rs, :])
        put(k, z + 1, r0, head, cond)
        ra_v[z, rs, :] = (po_v[z, rs, :] * sat - th_v[z, rs, :]) + sk_v[
            z // LEVELS_PER_LAYER, rs, :
        ]

    def second_half(z, c):
        for r0 in range(0, rows, CHUNK):
            rs = pl.ds(r0, CHUNK)
            resid = ra_v[z, rs, :] + sk_v[z // LEVELS_PER_LAYER, rs, :]
            curve_into(1, z, r0, p_v[z, rs, :] - resid * da_v[z, rs, :])
        return c

    def sweep_level(k, z, c):
        level = z + 1
        put_rows(k, level)
        for r0 in range(0, rows, CHUNK):
            rs = pl.ds(r0, CHUNK)
            head, flux, diag = stencil(k, level, r0)
            head = head - (ra_v[z, rs, :] + flux) * (OMEGAS[k] / diag)
            if k + 1 < SWEEPS:
                curve_into(k + 1, z, r0, head)
            else:
                out_p[z, rs, :] = head
        return c

    def run(k, body):
        lax.fori_loop(0, 2, lambda i, c: body(i * (levels - 1), c), 0)
        for copy in faces_z(k + 1):
            copy.start()
            started.append(copy)
        lax.fori_loop(1, levels - 1, body, 0)
        for copy in faces_xy(k + 1):
            copy.start()
            started.append(copy)

    run(0, second_half)
    lax.fori_loop(cut2, groups, land_start, 0)
    for k in range(1, SWEEPS):
        wait_faces(k)
        if k + 1 < SWEEPS:
            run(k, functools.partial(sweep_level, k))
        else:
            lax.fori_loop(0, levels, functools.partial(sweep_level, k), 0)

    for load in loads[8:]:
        load.wait()
    all_but_me = rx_v.at[pl.ds(0, (groups - 1) * per), :]
    pltpu.make_async_copy(all_but_me, all_but_me, land_recv).wait()
    sub = min(8, n_gx)
    n_layers = layers * n_gz
    for half in range(n_gx // sub):
        for r in range(CAP):
            b0 = half * sub

            def slots(ref, at3, stride):
                return ref[pl.ds(at3, sub, stride=stride), :]

            tpot = slots(tr_v, b0 * CAP + r, CAP)
            air = slots(ai_v, b0 * CAP + r, CAP)
            roots = slots(ro_v, b0 * CAP + r, CAP).astype(jnp.float32)
            weights = [root_weight(d, roots) for d in range(n_layers)]
            total = weights[0]
            for weight in weights[1:]:
                total = total + weight
            temps, kappa, upt = [], [], []
            for d in range(n_layers):
                bz, j = d // layers, d % layers
                base = (b0 * n_gz + bz) * per + r * tile + j
                lh = slots(rx_v, base, n_gz * per)
                ls = slots(rx_v, base + layers, n_gz * per)
                stress = 1.0 / (1.0 + lh * lh * (1.0 / 2.25))
                upt.append(0.3 * (tpot * (weights[d] / total) * stress))
                kappa.append(0.25 + 0.9 * ls)
                temps.append(slots(lt_v, (b0 * CAP + r) * n_layers + d, CAP * n_layers))
            mids = [0.5 * (kappa[d] + kappa[d + 1]) for d in range(n_layers - 1)]
            old = temps
            for _ in range(HEAT_STEPS):
                fresh = []
                for d in range(n_layers):
                    move = (
                        kappa[0] * (air - temps[0])
                        if d == 0
                        else mids[d - 1] * (temps[d - 1] - temps[d])
                    )
                    if d < n_layers - 1:
                        move = move + mids[d] * (temps[d + 1] - temps[d])
                    fresh.append(temps[d] + 0.2 * move - upt[d])
                temps = fresh
            filled = cnt_v[b0 : b0 + sub, :] > r
            for d in range(n_layers):
                out_lt[pl.ds((b0 * CAP + r) * n_layers + d, sub, stride=CAP * n_layers), :] = (
                    jnp.where(filled, temps[d], old[d])
                )

    for copy in started:
        copy.wait_send()
    drain(tp_v, n_gx - 1, zt_send)
    pltpu.make_async_copy(ref3, ref3, xt_send).wait()
    pltpu.make_async_copy(all_but_me, all_but_me, land_send).wait()


def solution(mesh):
    n_role, n_gx, n_gz = (mesh.shape[a] for a in ("role", "gx", "gz"))

    def local(p, al, vn, ks, po, owner, land, transp, air, roots):
        levels, rows, cols = p.shape
        layers = levels // LEVELS_PER_LAYER
        n_layers = layers * n_gz
        groups = n_gx * n_gz
        slots = n_gx * CAP
        f32 = jnp.float32
        cell = pltpu.VMEM((levels, rows, cols), f32)
        padded = pltpu.VMEM((SWEEPS, levels + 2, rows + 2 * PAD, cols), f32)
        xface = pltpu.VMEM((SWEEPS, 2, 2, levels, cols), f32)
        yface = pltpu.VMEM((SWEEPS, 2, rows, cols), f32)
        line = pltpu.VMEM((slots, cols), f32)
        payload = pltpu.VMEM((groups * CAP * 2 * layers, cols), f32)
        dma = pltpu.SemaphoreType.DMA
        head, temps = pl.pallas_call(
            functools.partial(kernel, n_role, n_gx, n_gz),
            out_shape=(
                jax.ShapeDtypeStruct(p.shape, f32),
                jax.ShapeDtypeStruct((slots * n_layers, cols), f32),
            ),
            in_specs=[pl.BlockSpec(memory_space=pl.ANY)] * 10,
            out_specs=[pl.BlockSpec(memory_space=pltpu.VMEM)] * 2,
            scratch_shapes=[
                cell,
                cell,
                cell,
                cell,
                cell,
                cell,
                cell,
                cell,
                cell,
                padded,
                padded,
                xface,
                xface,
                yface,
                yface,
                pltpu.VMEM(owner.shape[::-1], jnp.int32),
                pltpu.VMEM((slots * n_layers, cols), f32),
                line,
                line,
                pltpu.VMEM((slots, cols), jnp.int32),
                pltpu.VMEM((groups * CAP, 256), jnp.bfloat16),
                pltpu.VMEM((2 * rows, groups * 8), jnp.bfloat16),
                pltpu.VMEM((rows, cols), f32),
                pltpu.VMEM((n_gx, cols), f32),
                pltpu.VMEM((n_gx, 8, cols), f32),
                pltpu.VMEM((n_gx, n_gz, 8, cols), f32),
                pltpu.VMEM((rows, cols), f32),
                pltpu.VMEM((rows, cols), f32),
                pltpu.VMEM((layers, rows, cols), f32),
                pltpu.VMEM((layers, rows, cols), f32),
                pltpu.VMEM((layers, 256, 2 * cols), jnp.bfloat16),
                payload,
                payload,
                dma((10,)),
                dma,
                dma,
                dma,
                dma,
                dma((SWEEPS * 8,)),
                dma((SWEEPS * 8,)),
                dma,
                dma,
                pltpu.SemaphoreType.REGULAR,
            ],
            compiler_params=pltpu.CompilerParams(
                collective_id=0, has_side_effects=True, vmem_limit_bytes=56 * 1024 * 1024
            ),
        )(
            p,
            al,
            vn,
            ks,
            po,
            owner.T,
            land.reshape(slots * n_layers, cols),
            transp.reshape(slots, cols),
            air.reshape(slots, cols),
            roots.reshape(slots, cols),
        )
        return head, temps.reshape(land.shape)

    grid = P("gz", "gx", "role")
    slot = P("role", ("gx", "gz"), None, None)
    return jax.shard_map(
        local,
        mesh=mesh,
        in_specs=(grid,) * 5 + (P(), P("role", ("gx", "gz"), None, None, None)) + (slot,) * 3,
        out_specs=(grid, P("role", ("gx", "gz"), None, None, None)),
        check_vma=False,
    )
```

```python
import functools
import math

import jax
import jax.numpy as jnp
from jax import lax
from jax.experimental import pallas as pl
from jax.experimental.pallas import tpu as pltpu
from jax.sharding import PartitionSpec as P

LEVELS_PER_LAYER = 4
CAP = 3
SWEEPS = 3
HEAT_STEPS = 4
LOG2E = 1.0 / math.log(2.0)
CHUNK = 32
PARTS = 2
PAD = 8
MESH = pl.DeviceIdType.MESH
OMEGAS = [
    1.0 / (1.0 + 0.6 * math.cos(math.pi * (2 * k + 1) / (2 * SWEEPS))) for k in range(SWEEPS)
]


def curves(head, la, vn, m, ks):
    lx = vn * (la + (0.5 * LOG2E) * jnp.log(head * head + 0.01))
    soft = jnp.log(1.0 + jnp.exp2(lx)) * LOG2E
    root = jnp.exp2(-0.5 * (m * soft))
    gap = 1.0 - jnp.exp2(m * (lx - soft))
    return root * root, ks * root * (gap * gap)


def split3(x):
    hi = x.astype(jnp.bfloat16)
    rest = x - hi.astype(jnp.float32)
    mid = rest.astype(jnp.bfloat16)
    return hi, mid, (rest - mid.astype(jnp.float32)).astype(jnp.bfloat16)


def kernel(
    n_role,
    n_gx,
    n_gz,
    p_hbm,
    al_hbm,
    vn_hbm,
    ks_hbm,
    po_hbm,
    own_hbm,
    lt_hbm,
    tr_hbm,
    ai_hbm,
    ro_hbm,
    out_p,
    out_lt,
    la_v,
    vn_v,
    ks_v,
    po_v,
    m_v,
    th_v,
    ra_v,
    da_v,
    hp0,
    hp1,
    hp2,
    kp0,
    kp1,
    kp2,
    xs,
    xh,
    ys,
    yh,
    own_v,
    lt_v,
    tr_v,
    ai_v,
    ro_v,
    sel_v,
    get_v,
    act_v,
    cnt_v,
    tp_v,
    rt_v,
    tq_v,
    rq_v,
    sk_v,
    lh_v,
    mean_v,
    tx_v,
    rx_v,
    load_sem,
    zt_send,
    zt_recv,
    xt_send,
    xt_recv,
    h_send,
    h_recv,
    land_send,
    land_recv,
    line_sem,
):
    levels, rows, cols = p_hbm.shape
    layers = levels // LEVELS_PER_LAYER
    groups = n_gx * n_gz
    tile = 2 * layers
    per = CAP * tile
    role = lax.axis_index("role")
    gx = lax.axis_index("gx")
    gz = lax.axis_index("gz")
    me = gx * n_gz + gz
    hp = (hp0, hp1, hp2)
    kp = (kp0, kp1, kp2)
    half = levels // PARTS

    barrier = pltpu.get_barrier_semaphore()

    def greet_gx(i, c):
        pl.semaphore_signal(
            barrier, inc=1, device_id={"gx": lax.rem(gx + i, n_gx)}, device_id_type=MESH
        )
        return c

    def greet_gz(i, c):
        pl.semaphore_signal(
            barrier, inc=1, device_id={"gz": lax.rem(gz + i, n_gz)}, device_id_type=MESH
        )
        return c

    lax.fori_loop(1, n_gx, greet_gx, 0)
    lax.fori_loop(1, n_gz, greet_gz, 0)
    for step in (1, n_role - 1):
        pl.semaphore_signal(
            barrier, inc=1, device_id={"role": lax.rem(role + step, n_role)}, device_id_type=MESH
        )

    pairs = (
        (tr_hbm, tr_v),
        (ro_hbm, ro_v),
        (own_hbm, own_v),
        (p_hbm, hp0.at[pl.ds(1, levels), pl.ds(PAD, rows), :]),
        (al_hbm, la_v),
        (vn_hbm, vn_v),
        (ks_hbm, ks_v),
        (po_hbm, po_v),
        (lt_hbm, lt_v),
        (ai_hbm, ai_v),
    )
    loads = [pltpu.make_async_copy(a, b, load_sem.at[i]) for i, (a, b) in enumerate(pairs)]
    for load in loads:
        load.start()

    loads[0].wait()
    loads[1].wait()
    for b in range(n_gx):
        tp_v[b, CAP:4, :] = jnp.zeros((1, cols), jnp.float32)
        tp_v[b, 4 + CAP :, :] = jnp.zeros((1, cols), jnp.float32)
        tp_v[b, 0:CAP, :] = tr_v[b * CAP : (b + 1) * CAP, :]
        tp_v[b, 4 : 4 + CAP, :] = ro_v[b * CAP : (b + 1) * CAP, :].astype(jnp.float32)

    loads[2].wait()
    lane1 = lax.broadcasted_iota(jnp.int32, (1, 128), 1)
    sub4 = lax.broadcasted_iota(jnp.int32, (n_role, 128), 0)

    def role_lanes(start):
        return jnp.sum(
            jnp.where(sub4 == role, own_v[:, pl.ds(start, 128)], 0), axis=0, keepdims=True
        )

    pair = role_lanes(pl.multiple_of((gx // 2) * 128, 128))
    own = jnp.where(lax.rem(gx, 2) == 1, pltpu.roll(pair, 64, 1), pair)
    ii = lax.broadcasted_iota(jnp.int32, (128, 128), 0)
    jj = lax.broadcasted_iota(jnp.int32, (128, 128), 1)
    by_lane = jnp.broadcast_to(own, (128, 128))
    by_sub = jnp.transpose(by_lane)
    earlier = (by_lane == by_sub) & (ii < jj) & (ii < rows)
    rank_lane = jnp.sum(jnp.where(earlier, 1, 0), axis=0, keepdims=True)
    rank_sub = jnp.transpose(jnp.broadcast_to(rank_lane, (128, 128)))
    key = jnp.where((own >= 0) & (lane1 < rows), own * CAP + rank_lane + 1, 0)
    key = jnp.broadcast_to(key + pltpu.roll(key, 64, 1), (groups * CAP, 128))
    slot = lax.broadcasted_iota(jnp.int32, (groups * CAP, 128), 0) + 1
    wide = lax.broadcasted_iota(jnp.int32, (groups * CAP, 128), 1)
    pick = key == slot
    sel_v[:, 0:128] = jnp.where(pick, 1.0, 0.0).astype(jnp.bfloat16)
    sel_v[:, 128:256] = jnp.where(pick & (wide < rows), 1.0, 0.0).astype(jnp.bfloat16)
    at = jnp.where(by_sub >= 0, by_sub * 8 + rank_sub, -8)[:rows]
    width = min(128, groups * 8)
    for t in range(groups * 8 // width):
        for f in range(2):
            hit = at + 4 * f == jj[:rows] + t * width
            get_v[f * rows : (f + 1) * rows, t * width : (t + 1) * width] = jnp.where(
                hit[:, :width], 1.0, 0.0
            ).astype(jnp.bfloat16)
    act_v[...] = jnp.where(by_sub[:rows] >= 0, 1.0, 0.0)
    for t in range(n_gx // 2):
        hit = jnp.where(role_lanes(t * 128) == me, 1.0, 0.0)
        for side in range(2):
            part = jnp.where((lane1 < 64) == (side == 0), hit, 0.0)
            cnt_v[2 * t + side : 2 * t + side + 1, :] = jnp.broadcast_to(
                jnp.sum(part, axis=1, keepdims=True), (1, 128)
            )

    lane = lax.broadcasted_iota(jnp.int32, (8, 128), 1)
    wide_lane = lax.broadcasted_iota(jnp.int32, (CHUNK, 128), 1)

    def pack_y(k, d, part, r0, at0, head, cond):
        face = ys[k, d, part]
        for g in range(r0 // 8, (r0 + CHUNK) // 8):
            for f, ref in enumerate((head, cond)):
                to = g * 16 + f * half + at0
                shift = to if d == 0 else jnp.bitwise_and(to + 1, 127)
                face = jnp.where(
                    lane == to, pltpu.roll(ref[g * 8 - r0 : g * 8 - r0 + 8], shift, 1), face
                )
        ys[k, d, part] = face

    def take_y(k, d, part, r0, at0, f):
        face = yh[k, d, part]
        end = 128 if d == 0 else 127
        return jnp.concatenate(
            [
                pltpu.roll(face, end - g * 16 - f * half - at0, 1)
                for g in range(r0 // 8, (r0 + CHUNK) // 8)
            ],
            axis=0,
        )

    def put(k, part, z, r0, head, cond, keep_head=True):
        if keep_head:
            hp[k][z + 1, pl.ds(PAD + r0, CHUNK), :] = head
        kp[k][z + 1, pl.ds(PAD + r0, CHUNK), :] = cond
        at0 = z - part * half
        if r0 == 0:
            xs[k, 0, part, 0, pl.ds(at0, 1), :] = head[0:1]
            xs[k, 0, part, 1, pl.ds(at0, 1), :] = cond[0:1]
        if r0 + CHUNK == rows:
            xs[k, 1, part, 0, pl.ds(at0, 1), :] = head[CHUNK - 1 :]
            xs[k, 1, part, 1, pl.ds(at0, 1), :] = cond[CHUNK - 1 :]
        for d in range(2):
            pack_y(k, d, part, r0, at0, head, cond)

    def remote(src, dst, k, slot, dst_slot, where):
        return pltpu.make_async_remote_copy(
            src_ref=src,
            dst_ref=dst,
            send_sem=h_send.at[k * 12 + slot],
            recv_sem=h_recv.at[k * 12 + dst_slot],
            device_id=where,
            device_id_type=MESH,
        )

    started = []

    def send(copies):
        for copy in copies:
            copy.start()
        started.extend(copies)

    def face_z(k, d):
        to = lax.rem(gz + (n_gz - 1 if d == 0 else 1), n_gz)
        made = []
        for f, ref in enumerate((hp[k], kp[k])):
            src = ref.at[1 if d == 0 else levels, pl.ds(PAD, rows), :]
            dst = ref.at[levels + 1 if d == 0 else 0, pl.ds(PAD, rows), :]
            made.append(remote(src, dst, k, 8 + 2 * f + d, 8 + 2 * f + 1 - d, {"gz": to}))
        return made

    def faces_xy(k, part):
        made = []
        for d in range(2):
            to = lax.rem(gx + (n_gx - 1 if d == 0 else 1), n_gx)
            made.append(
                remote(
                    xs.at[k, d, part],
                    xh.at[k, 1 - d, part],
                    k,
                    2 * part + d,
                    2 * part + 1 - d,
                    {"gx": to},
                )
            )
        for d in range(2):
            to = lax.rem(role + (n_role - 1 if d == 0 else 1), n_role)
            made.append(
                remote(
                    ys.at[k, d, part],
                    yh.at[k, 1 - d, part],
                    k,
                    4 + 2 * part + d,
                    4 + 2 * part + 1 - d,
                    {"role": to},
                )
            )
        return made

    mean_v[:, CAP * rows :, :] = jnp.zeros((layers, 256 - CAP * rows, 2 * cols), jnp.bfloat16)
    for load in loads[3:8]:
        load.wait()

    def start_layer(part, i, c):
        j = part * (layers // PARTS) + (layers // PARTS - 1 - i)
        for r0 in range(0, rows, CHUNK):
            rs = pl.ds(r0, CHUNK)
            sum_s = None
            sum_h = None
            for i in range(LEVELS_PER_LAYER):
                z = j * LEVELS_PER_LAYER + i
                head = hp[0][z + 1, pl.ds(PAD + r0, CHUNK), :]
                vn = vn_v[z, rs, :]
                la = jnp.log(la_v[z, rs, :]) * LOG2E
                m = 1.0 - 1.0 / vn
                la_v[z, rs, :] = la
                m_v[z, rs, :] = m
                sat, cond = curves(head, la, vn, m, ks_v[z, rs, :])
                th_v[z, rs, :] = po_v[z, rs, :] * sat
                put(0, part, z, r0, head, cond, keep_head=False)
                sum_s = sat if sum_s is None else sum_s + sat
                sum_h = head if sum_h is None else sum_h + head
            mean_h = sum_h * 0.25
            lh_v[j, rs, :] = mean_h
            for f, mean in enumerate((mean_h, sum_s * 0.25)):
                for piece, value in enumerate(split3(mean)):
                    mean_v[
                        j,
                        piece * rows + r0 : piece * rows + r0 + CHUNK,
                        f * cols : (f + 1) * cols,
                    ] = value
        return c

    lax.fori_loop(0, layers // PARTS, functools.partial(start_layer, 0), 0)

    pl.semaphore_wait(barrier, (n_gx - 1) + (n_gz - 1) + 2)

    def tell_line(i, c):
        pl.semaphore_signal(
            line_sem, inc=1, device_id={"gz": lax.rem(gz + i, n_gz)}, device_id_type=MESH
        )
        return c

    lax.fori_loop(1, n_gz, tell_line, 0)

    def zt_copy(i):
        to = lax.rem(gx + i, n_gx)
        return pltpu.make_async_remote_copy(
            src_ref=tp_v.at[to],
            dst_ref=rt_v.at[gx, gz],
            send_sem=zt_send,
            recv_sem=zt_recv,
            device_id={"gx": to},
            device_id_type=MESH,
        )

    def zt_start(i, c):
        zt_copy(i).start()
        return c

    lax.fori_loop(1, n_gx, zt_start, 0)
    rt_v[gx, gz] = tp_v[gx]

    send(face_z(0, 0) + faces_xy(0, 0))
    lax.fori_loop(0, layers // PARTS, functools.partial(start_layer, 1), 0)
    send(face_z(0, 1) + faces_xy(0, 1))

    for j in range(layers):
        out = jnp.dot(sel_v[...], mean_v[j], preferred_element_type=jnp.float32)
        tx_v[pl.ds(j, groups * CAP, stride=tile), :] = out[:, :cols]
        tx_v[pl.ds(layers + j, groups * CAP, stride=tile), :] = out[:, cols:]
    rx_v[pl.ds(pl.multiple_of(me * per, 8), per), :] = tx_v[
        pl.ds(pl.multiple_of(me * per, 8), per), :
    ]
    pl.semaphore_wait(line_sem, n_gz - 1)

    def land_start(i, c):
        to_gx = lax.rem(gx + i // n_gz, n_gx)
        to_gz = lax.rem(gz + lax.rem(i, n_gz), n_gz)
        to = to_gx * n_gz + to_gz
        pltpu.make_async_remote_copy(
            src_ref=tx_v.at[pl.ds(pl.multiple_of(to * per, 8), per), :],
            dst_ref=rx_v.at[pl.ds(pl.multiple_of(me * per, 8), per), :],
            send_sem=land_send,
            recv_sem=land_recv,
            device_id={"gx": to_gx, "gz": to_gz},
            device_id_type=MESH,
        ).start()
        return c

    cut1 = groups // 4
    cut2 = groups // 2
    lax.fori_loop(1, cut1, land_start, 0)

    def drain(ref, count, sem):
        pltpu.make_async_copy(ref.at[pl.ds(0, count)], ref.at[pl.ds(0, count)], sem).wait()

    drain(tp_v, n_gx - 1, zt_recv)

    def xt_copy(i):
        return pltpu.make_async_remote_copy(
            src_ref=rt_v.at[:, gz],
            dst_ref=rt_v.at[:, gz],
            send_sem=xt_send,
            recv_sem=xt_recv,
            device_id={"gz": lax.rem(gz + i, n_gz)},
            device_id_type=MESH,
        )

    for i in range(1, n_gz):
        xt_copy(i).start()

    sign = jnp.where(jnp.bitwise_and(lane, 15) < half, 1.0, -1.0)

    def wait_part(k, part):
        views = [(2 * part + d, xh.at[k, d, part]) for d in range(2)]
        views += [(4 + 2 * part + d, yh.at[k, d, part]) for d in range(2)]
        plane, edge = (0, 1) if part == 0 else (levels + 1, levels)
        for f, ref in enumerate((hp[k], kp[k])):
            views.append((8 + 2 * f + part, ref.at[plane, pl.ds(PAD, rows), :]))
        for slot, view in views:
            pltpu.make_async_copy(view, view, h_recv.at[k * 12 + slot]).wait()

        @pl.when(gz == (0 if part == 0 else n_gz - 1))
        def _():
            hp[k][plane, pl.ds(PAD, rows), :] = hp[k][edge, pl.ds(PAD, rows), :]
            kp[k][plane, pl.ds(PAD, rows), :] = -kp[k][edge, pl.ds(PAD, rows), :]

        for d in range(2):

            @pl.when(role == (0 if d == 0 else n_role - 1))
            def _():
                yh[k, d, part] = ys[k, d, part] * sign

            @pl.when(gx == (0 if d == 0 else n_gx - 1))
            def _():
                xh[k, d, part, 0] = xs[k, d, part, 0]
                xh[k, d, part, 1] = -xs[k, d, part, 1]

        for d, row in ((0, PAD - 1), (1, PAD + rows)):
            for f, ref in enumerate((hp[k], kp[k])):
                for i in range(half):
                    z = part * half + i
                    ref[z + 1, row : row + 1, :] = xh[k, d, part, f, i : i + 1, :]

    def stencil(k, part, z, r0):
        def cut(ref, plane, shift):
            return ref[k][plane, pl.ds(PAD + r0 + shift, CHUNK), :]

        at0 = z - part * half
        h, c = cut(hp, z + 1, 0), cut(kp, z + 1, 0)
        first, last = wide_lane == 0, wide_lane == 127
        c_ym = jnp.where(first, take_y(k, 0, part, r0, at0, 1), pltpu.roll(c, 1, 1))
        c_yp = jnp.where(last, take_y(k, 1, part, r0, at0, 1), pltpu.roll(c, 127, 1))
        h_ym = jnp.where(first, take_y(k, 0, part, r0, at0, 0), pltpu.roll(h, 1, 1))
        h_yp = jnp.where(last, take_y(k, 1, part, r0, at0, 0), pltpu.roll(h, 127, 1))
        c_up, c_dn = cut(kp, z, 0), cut(kp, z + 2, 0)
        kf_up = c + c_up
        kf_dn = c + c_dn
        kf_xm = c + cut(kp, z + 1, -1)
        kf_xp = c + cut(kp, z + 1, 1)
        kf_ym = c + c_ym
        kf_yp = c + c_yp
        flux = kf_up * (h - cut(hp, z, 0)) + kf_dn * (h - cut(hp, z + 2, 0))
        flux = flux + kf_xm * (h - cut(hp, z + 1, -1)) + kf_xp * (h - cut(hp, z + 1, 1))
        flux = flux + kf_ym * (h - h_ym) + kf_yp * (h - h_yp)
        diag = 2.0 + ((kf_up + kf_dn) + (kf_xm + kf_xp) + (kf_ym + kf_yp))
        return h, flux + (c_dn - c_up), diag

    def first_half(part, i, c):
        z = part * half + (half - 1 - i)
        for r0 in range(0, rows, CHUNK):
            _, resid, diag = stencil(0, part, z, r0)
            ra_v[z, pl.ds(r0, CHUNK), :] = resid
            da_v[z, pl.ds(r0, CHUNK), :] = OMEGAS[0] / diag
        return c

    for part in range(PARTS):
        wait_part(0, part)
        lax.fori_loop(0, half, functools.partial(first_half, part), 0)
    lax.fori_loop(cut1, cut2, land_start, 0)

    ref3 = rt_v.at[:, pl.ds(0, n_gz - 1)]
    pltpu.make_async_copy(ref3, ref3, xt_recv).wait()

    pieces = jnp.concatenate(split3(rt_v[...].reshape(groups * 8, cols)), axis=1)
    got = jnp.dot(get_v[...], pieces, preferred_element_type=jnp.float32)
    got = got[:, :cols] + got[:, cols : 2 * cols] + got[:, 2 * cols :]
    tq_v[...] = got[:rows]
    rq_v[...] = got[rows:] + (1.0 - act_v[...])

    def root_weight(depth, roots):
        return jnp.where(depth < roots, math.exp(-depth / 4.0), 0.0)

    for r0 in range(0, rows, CHUNK):
        rs = pl.ds(r0, CHUNK)
        roots = rq_v[rs, :]
        total = root_weight(0, roots)
        for depth in range(1, layers * n_gz):
            total = total + root_weight(depth, roots)
        scale = tq_v[rs, :]
        for j in range(layers):
            depth = (gz * layers + j).astype(jnp.float32)
            weight = jnp.where(
                depth < roots, jnp.exp(jnp.full((CHUNK, 128), -0.25, jnp.float32) * depth), 0.0
            )
            lh = lh_v[j, rs, :]
            stress = 1.0 / (1.0 + lh * lh * (1.0 / 2.25))
            sk_v[j, rs, :] = 2.0 * (scale * (weight / total) * stress)

    def curve_into(k, part, z, r0, head):
        rs = pl.ds(r0, CHUNK)
        sat, cond = curves(head, la_v[z, rs, :], vn_v[z, rs, :], m_v[z, rs, :], ks_v[z, rs, :])
        put(k, part, z, r0, head, cond)
        gain = po_v[z, rs, :] * sat - th_v[z, rs, :]
        ra_v[z, rs, :] = (gain + gain) + sk_v[z // LEVELS_PER_LAYER, rs, :]

    def second_half(part, i, c):
        z = part * half + (half - 1 - i)
        for r0 in range(0, rows, CHUNK):
            rs = pl.ds(r0, CHUNK)
            resid = ra_v[z, rs, :] + sk_v[z // LEVELS_PER_LAYER, rs, :]
            head = hp[0][z + 1, pl.ds(PAD + r0, CHUNK), :]
            curve_into(1, part, z, r0, head - resid * da_v[z, rs, :])
        return c

    def sweep_level(k, part, i, c):
        z = part * half + (half - 1 - i)
        for r0 in range(0, rows, CHUNK):
            rs = pl.ds(r0, CHUNK)
            head, flux, diag = stencil(k, part, z, r0)
            head = head - (ra_v[z, rs, :] + flux) * (OMEGAS[k] / diag)
            if k + 1 < SWEEPS:
                curve_into(k + 1, part, z, r0, head)
            else:
                out_p[z, rs, :] = head
        return c

    for part in range(PARTS):
        lax.fori_loop(0, half, functools.partial(second_half, part), 0)
        send(face_z(1, part) + faces_xy(1, part))
    lax.fori_loop(cut2, groups, land_start, 0)
    for k in range(1, SWEEPS):
        for part in range(PARTS):
            wait_part(k, part)
            lax.fori_loop(0, half, functools.partial(sweep_level, k, part), 0)
            if k + 1 < SWEEPS:
                send(face_z(k + 1, part) + faces_xy(k + 1, part))

    for load in loads[8:]:
        load.wait()
    all_but_me = rx_v.at[pl.ds(0, (groups - 1) * per), :]
    pltpu.make_async_copy(all_but_me, all_but_me, land_recv).wait()
    sub = min(8, n_gx)
    n_layers = layers * n_gz
    for block in range(n_gx // sub):
        for r in range(CAP):
            b0 = block * sub

            def slots(ref, at3, stride):
                return ref[pl.ds(at3, sub, stride=stride), :]

            tpot = slots(tr_v, b0 * CAP + r, CAP)
            air = slots(ai_v, b0 * CAP + r, CAP)
            roots = slots(ro_v, b0 * CAP + r, CAP).astype(jnp.float32)
            weights = [root_weight(d, roots) for d in range(n_layers)]
            total = weights[0]
            for weight in weights[1:]:
                total = total + weight
            temps, kappa, upt = [], [], []
            for d in range(n_layers):
                bz, j = d // layers, d % layers
                base = (b0 * n_gz + bz) * per + r * tile + j
                lh = slots(rx_v, base, n_gz * per)
                ls = slots(rx_v, base + layers, n_gz * per)
                stress = 1.0 / (1.0 + lh * lh * (1.0 / 2.25))
                upt.append(0.3 * (tpot * (weights[d] / total) * stress))
                kappa.append(0.25 + 0.9 * ls)
                temps.append(slots(lt_v, (b0 * CAP + r) * n_layers + d, CAP * n_layers))
            mids = [0.5 * (kappa[d] + kappa[d + 1]) for d in range(n_layers - 1)]
            old = temps
            for _ in range(HEAT_STEPS):
                fresh = []
                for d in range(n_layers):
                    move = (
                        kappa[0] * (air - temps[0])
                        if d == 0
                        else mids[d - 1] * (temps[d - 1] - temps[d])
                    )
                    if d < n_layers - 1:
                        move = move + mids[d] * (temps[d + 1] - temps[d])
                    fresh.append(temps[d] + 0.2 * move - upt[d])
                temps = fresh
            filled = cnt_v[b0 : b0 + sub, :] > r
            for d in range(n_layers):
                out_lt[pl.ds((b0 * CAP + r) * n_layers + d, sub, stride=CAP * n_layers), :] = (
                    jnp.where(filled, temps[d], old[d])
                )

    for copy in started:
        copy.wait_send()
    drain(tp_v, n_gx - 1, zt_send)
    pltpu.make_async_copy(ref3, ref3, xt_send).wait()
    pltpu.make_async_copy(all_but_me, all_but_me, land_send).wait()


def solution(mesh):
    n_role, n_gx, n_gz = (mesh.shape[a] for a in ("role", "gx", "gz"))

    def local(p, al, vn, ks, po, owner, land, transp, air, roots):
        levels, rows, cols = p.shape
        layers = levels // LEVELS_PER_LAYER
        n_layers = layers * n_gz
        groups = n_gx * n_gz
        slots = n_gx * CAP
        f32 = jnp.float32
        cell = pltpu.VMEM((levels, rows, cols), f32)
        padded = pltpu.VMEM((levels + 2, rows + 2 * PAD, cols), f32)
        xface = pltpu.VMEM((SWEEPS, 2, PARTS, 2, levels // PARTS, cols), f32)
        yface = pltpu.VMEM((SWEEPS, 2, PARTS, 8, cols), f32)
        line = pltpu.VMEM((slots, cols), f32)
        payload = pltpu.VMEM((groups * CAP * 2 * layers, cols), f32)
        dma = pltpu.SemaphoreType.DMA
        head, temps = pl.pallas_call(
            functools.partial(kernel, n_role, n_gx, n_gz),
            out_shape=(
                jax.ShapeDtypeStruct(p.shape, f32),
                jax.ShapeDtypeStruct((slots * n_layers, cols), f32),
            ),
            in_specs=[pl.BlockSpec(memory_space=pl.ANY)] * 10,
            out_specs=[pl.BlockSpec(memory_space=pltpu.VMEM)] * 2,
            scratch_shapes=[
                cell,
                cell,
                cell,
                cell,
                cell,
                cell,
                cell,
                cell,
                padded,
                padded,
                padded,
                padded,
                padded,
                padded,
                xface,
                xface,
                yface,
                yface,
                pltpu.VMEM(owner.shape[::-1], jnp.int32),
                pltpu.VMEM((slots * n_layers, cols), f32),
                line,
                line,
                pltpu.VMEM((slots, cols), jnp.int32),
                pltpu.VMEM((groups * CAP, 256), jnp.bfloat16),
                pltpu.VMEM((2 * rows, groups * 8), jnp.bfloat16),
                pltpu.VMEM((rows, cols), f32),
                pltpu.VMEM((n_gx, cols), f32),
                pltpu.VMEM((n_gx, 8, cols), f32),
                pltpu.VMEM((n_gx, n_gz, 8, cols), f32),
                pltpu.VMEM((rows, cols), f32),
                pltpu.VMEM((rows, cols), f32),
                pltpu.VMEM((layers, rows, cols), f32),
                pltpu.VMEM((layers, rows, cols), f32),
                pltpu.VMEM((layers, 256, 2 * cols), jnp.bfloat16),
                payload,
                payload,
                dma((10,)),
                dma,
                dma,
                dma,
                dma,
                dma((SWEEPS * 12,)),
                dma((SWEEPS * 12,)),
                dma,
                dma,
                pltpu.SemaphoreType.REGULAR,
            ],
            compiler_params=pltpu.CompilerParams(
                collective_id=0, has_side_effects=True, vmem_limit_bytes=56 * 1024 * 1024
            ),
        )(
            p,
            al,
            vn,
            ks,
            po,
            owner.T,
            land.reshape(slots * n_layers, cols),
            transp.reshape(slots, cols),
            air.reshape(slots, cols),
            roots.reshape(slots, cols),
        )
        return head, temps.reshape(land.shape)

    grid = P("gz", "gx", "role")
    slot = P("role", ("gx", "gz"), None, None)
    return jax.shard_map(
        local,
        mesh=mesh,
        in_specs=(grid,) * 5 + (P(), P("role", ("gx", "gz"), None, None, None)) + (slot,) * 3,
        out_specs=(grid, P("role", ("gx", "gz"), None, None, None)),
        check_vma=False,
    )
```

```python
import functools
import math

import jax
import jax.numpy as jnp
from jax import lax
from jax.experimental import pallas as pl
from jax.experimental.pallas import tpu as pltpu
from jax.sharding import PartitionSpec as P

LEVELS_PER_LAYER = 4
CAP = 3
SWEEPS = 3
HEAT_STEPS = 4
LOG2E = 1.0 / math.log(2.0)
CHUNK = 32
PARTS = 2
PACE = (48, 0)
PAD = 8
MESH = pl.DeviceIdType.MESH
OMEGAS = [
    1.0 / (1.0 + 0.6 * math.cos(math.pi * (2 * k + 1) / (2 * SWEEPS))) for k in range(SWEEPS)
]


def curves(head, la, vn, m, ks):
    lx = vn * (la + (0.5 * LOG2E) * jnp.log(head * head + 0.01))
    soft = jnp.log(1.0 + jnp.exp2(lx)) * LOG2E
    root = jnp.exp2(-0.5 * (m * soft))
    gap = 1.0 - jnp.exp2(m * (lx - soft))
    return root * root, ks * root * (gap * gap)


def split3(x):
    hi = x.astype(jnp.bfloat16)
    rest = x - hi.astype(jnp.float32)
    mid = rest.astype(jnp.bfloat16)
    return hi, mid, (rest - mid.astype(jnp.float32)).astype(jnp.bfloat16)


def kernel(
    n_role,
    n_gx,
    n_gz,
    p_hbm,
    al_hbm,
    vn_hbm,
    ks_hbm,
    po_hbm,
    own_hbm,
    lt_hbm,
    tr_hbm,
    ai_hbm,
    ro_hbm,
    out_p,
    out_lt,
    la_v,
    vn_v,
    ks_v,
    po_v,
    m_v,
    th_v,
    ra_v,
    da_v,
    hp0,
    hp1,
    hp2,
    kp0,
    kp1,
    kp2,
    xs,
    xh,
    ys,
    yh,
    own_v,
    lt_v,
    tr_v,
    ai_v,
    ro_v,
    sel_v,
    get_v,
    act_v,
    cnt_v,
    tp_v,
    rt_v,
    tq_v,
    rq_v,
    sk_v,
    lh_v,
    mean_v,
    tx_v,
    rx_v,
    load_sem,
    zt_send,
    zt_recv,
    xt_send,
    xt_recv,
    h_send,
    h_recv,
    land_send,
    land_recv,
    line_sem,
):
    levels, rows, cols = p_hbm.shape
    layers = levels // LEVELS_PER_LAYER
    groups = n_gx * n_gz
    tile = 2 * layers
    per = CAP * tile
    role = lax.axis_index("role")
    gx = lax.axis_index("gx")
    gz = lax.axis_index("gz")
    me = gx * n_gz + gz
    hp = (hp0, hp1, hp2)
    kp = (kp0, kp1, kp2)
    half = levels // PARTS

    barrier = pltpu.get_barrier_semaphore()

    def greet_gx(i, c):
        pl.semaphore_signal(
            barrier, inc=1, device_id={"gx": lax.rem(gx + i, n_gx)}, device_id_type=MESH
        )
        return c

    def greet_gz(i, c):
        pl.semaphore_signal(
            barrier, inc=1, device_id={"gz": lax.rem(gz + i, n_gz)}, device_id_type=MESH
        )
        return c

    lax.fori_loop(1, n_gx, greet_gx, 0)
    lax.fori_loop(1, n_gz, greet_gz, 0)
    for step in (1, n_role - 1):
        pl.semaphore_signal(
            barrier, inc=1, device_id={"role": lax.rem(role + step, n_role)}, device_id_type=MESH
        )

    pairs = (
        (tr_hbm, tr_v),
        (ro_hbm, ro_v),
        (own_hbm, own_v),
        (p_hbm, hp0.at[pl.ds(1, levels), pl.ds(PAD, rows), :]),
        (al_hbm, la_v),
        (vn_hbm, vn_v),
        (ks_hbm, ks_v),
        (po_hbm, po_v),
        (lt_hbm, lt_v),
        (ai_hbm, ai_v),
    )
    loads = [pltpu.make_async_copy(a, b, load_sem.at[i]) for i, (a, b) in enumerate(pairs)]
    for load in loads:
        load.start()

    loads[0].wait()
    loads[1].wait()
    for b in range(n_gx):
        tp_v[b, CAP:4, :] = jnp.zeros((1, cols), jnp.float32)
        tp_v[b, 4 + CAP :, :] = jnp.zeros((1, cols), jnp.float32)
        tp_v[b, 0:CAP, :] = tr_v[b * CAP : (b + 1) * CAP, :]
        tp_v[b, 4 : 4 + CAP, :] = ro_v[b * CAP : (b + 1) * CAP, :].astype(jnp.float32)

    loads[2].wait()
    lane1 = lax.broadcasted_iota(jnp.int32, (1, 128), 1)
    sub4 = lax.broadcasted_iota(jnp.int32, (n_role, 128), 0)

    def role_lanes(start):
        return jnp.sum(
            jnp.where(sub4 == role, own_v[:, pl.ds(start, 128)], 0), axis=0, keepdims=True
        )

    pair = role_lanes(pl.multiple_of((gx // 2) * 128, 128))
    own = jnp.where(lax.rem(gx, 2) == 1, pltpu.roll(pair, 64, 1), pair)
    ii = lax.broadcasted_iota(jnp.int32, (128, 128), 0)
    jj = lax.broadcasted_iota(jnp.int32, (128, 128), 1)
    by_lane = jnp.broadcast_to(own, (128, 128))
    by_sub = jnp.transpose(by_lane)
    earlier = (by_lane == by_sub) & (ii < jj) & (ii < rows)
    rank_lane = jnp.sum(jnp.where(earlier, 1, 0), axis=0, keepdims=True)
    rank_sub = jnp.transpose(jnp.broadcast_to(rank_lane, (128, 128)))
    key = jnp.where((own >= 0) & (lane1 < rows), own * CAP + rank_lane + 1, 0)
    key = jnp.broadcast_to(key + pltpu.roll(key, 64, 1), (groups * CAP, 128))
    slot = lax.broadcasted_iota(jnp.int32, (groups * CAP, 128), 0) + 1
    wide = lax.broadcasted_iota(jnp.int32, (groups * CAP, 128), 1)
    pick = key == slot
    sel_v[:, 0:128] = jnp.where(pick, 1.0, 0.0).astype(jnp.bfloat16)
    sel_v[:, 128:256] = jnp.where(pick & (wide < rows), 1.0, 0.0).astype(jnp.bfloat16)
    at = jnp.where(by_sub >= 0, by_sub * 8 + rank_sub, -8)[:rows]
    width = min(128, groups * 8)
    for t in range(groups * 8 // width):
        for f in range(2):
            hit = at + 4 * f == jj[:rows] + t * width
            get_v[f * rows : (f + 1) * rows, t * width : (t + 1) * width] = jnp.where(
                hit[:, :width], 1.0, 0.0
            ).astype(jnp.bfloat16)
    act_v[...] = jnp.where(by_sub[:rows] >= 0, 1.0, 0.0)
    for t in range(n_gx // 2):
        hit = jnp.where(role_lanes(t * 128) == me, 1.0, 0.0)
        for side in range(2):
            part = jnp.where((lane1 < 64) == (side == 0), hit, 0.0)
            cnt_v[2 * t + side : 2 * t + side + 1, :] = jnp.broadcast_to(
                jnp.sum(part, axis=1, keepdims=True), (1, 128)
            )

    segments = (
        ((0, 2, lambda i: i * (levels - 1)), (2, half, lambda i: i - 1)),
        ((0, half, lambda i: half - 1 + i),),
    )

    def level_at(part, i):
        return next(at(i) for begin, end, at in segments[part] if begin <= i < end)

    def place_of(z):
        if z in (0, levels - 1):
            return 0, min(z, 1)
        return (0, z + 1) if z < half - 1 else (1, z - half + 1)

    lane = lax.broadcasted_iota(jnp.int32, (8, 128), 1)
    wide_lane = lax.broadcasted_iota(jnp.int32, (CHUNK, 128), 1)

    def pack_y(k, d, part, r0, at0, head, cond):
        face = ys[k, d, part]
        for g in range(r0 // 8, (r0 + CHUNK) // 8):
            for f, ref in enumerate((head, cond)):
                to = g * 16 + f * half + at0
                shift = to if d == 0 else jnp.bitwise_and(to + 1, 127)
                face = jnp.where(
                    lane == to, pltpu.roll(ref[g * 8 - r0 : g * 8 - r0 + 8], shift, 1), face
                )
        ys[k, d, part] = face

    def take_y(k, d, part, r0, at0, f):
        face = yh[k, d, part]
        end = 128 if d == 0 else 127
        return jnp.concatenate(
            [
                pltpu.roll(face, end - g * 16 - f * half - at0, 1)
                for g in range(r0 // 8, (r0 + CHUNK) // 8)
            ],
            axis=0,
        )

    def put(k, part, at0, z, r0, head, cond, keep_head=True):
        if keep_head:
            hp[k][z + 1, pl.ds(PAD + r0, CHUNK), :] = head
        kp[k][z + 1, pl.ds(PAD + r0, CHUNK), :] = cond
        if r0 == 0:
            xs[k, 0, part, 0, pl.ds(at0, 1), :] = head[0:1]
            xs[k, 0, part, 1, pl.ds(at0, 1), :] = cond[0:1]
        if r0 + CHUNK == rows:
            xs[k, 1, part, 0, pl.ds(at0, 1), :] = head[CHUNK - 1 :]
            xs[k, 1, part, 1, pl.ds(at0, 1), :] = cond[CHUNK - 1 :]
        for d in range(2):
            pack_y(k, d, part, r0, at0, head, cond)

    def remote(src, dst, k, slot, dst_slot, where):
        return pltpu.make_async_remote_copy(
            src_ref=src,
            dst_ref=dst,
            send_sem=h_send.at[k * 12 + slot],
            recv_sem=h_recv.at[k * 12 + dst_slot],
            device_id=where,
            device_id_type=MESH,
        )

    started = []

    def send(copies):
        for copy in copies:
            copy.start()
        started.extend(copies)

    def face_z(k, d):
        to = lax.rem(gz + (n_gz - 1 if d == 0 else 1), n_gz)
        made = []
        for f, ref in enumerate((hp[k], kp[k])):
            src = ref.at[1 if d == 0 else levels, pl.ds(PAD, rows), :]
            dst = ref.at[levels + 1 if d == 0 else 0, pl.ds(PAD, rows), :]
            made.append(remote(src, dst, k, 8 + 2 * f + d, 8 + 2 * f + 1 - d, {"gz": to}))
        return made

    def faces_xy(k, part):
        made = []
        for d in range(2):
            to = lax.rem(gx + (n_gx - 1 if d == 0 else 1), n_gx)
            made.append(
                remote(
                    xs.at[k, d, part],
                    xh.at[k, 1 - d, part],
                    k,
                    2 * part + d,
                    2 * part + 1 - d,
                    {"gx": to},
                )
            )
        for d in range(2):
            to = lax.rem(role + (n_role - 1 if d == 0 else 1), n_role)
            made.append(
                remote(
                    ys.at[k, d, part],
                    yh.at[k, 1 - d, part],
                    k,
                    4 + 2 * part + d,
                    4 + 2 * part + 1 - d,
                    {"role": to},
                )
            )
        return made

    mean_v[:, CAP * rows :, :] = jnp.zeros((layers, 256 - CAP * rows, 2 * cols), jnp.bfloat16)
    for load in loads[3:8]:
        load.wait()

    def start_layer(j):
        for r0 in range(0, rows, CHUNK):
            rs = pl.ds(r0, CHUNK)
            sum_s = None
            sum_h = None
            for i in range(LEVELS_PER_LAYER):
                z = j * LEVELS_PER_LAYER + i
                head = hp[0][z + 1, pl.ds(PAD + r0, CHUNK), :]
                vn = vn_v[z, rs, :]
                la = jnp.log(la_v[z, rs, :]) * LOG2E
                m = 1.0 - 1.0 / vn
                la_v[z, rs, :] = la
                m_v[z, rs, :] = m
                sat, cond = curves(head, la, vn, m, ks_v[z, rs, :])
                th_v[z, rs, :] = po_v[z, rs, :] * sat
                part, at0 = place_of(z)
                put(0, part, at0, z, r0, head, cond, keep_head=False)
                sum_s = sat if sum_s is None else sum_s + sat
                sum_h = head if sum_h is None else sum_h + head
            mean_h = sum_h * 0.25
            lh_v[j, rs, :] = mean_h
            for f, mean in enumerate((mean_h, sum_s * 0.25)):
                for piece, value in enumerate(split3(mean)):
                    mean_v[
                        j,
                        piece * rows + r0 : piece * rows + r0 + CHUNK,
                        f * cols : (f + 1) * cols,
                    ] = value

    start_layer(0)
    start_layer(layers - 1)

    pl.semaphore_wait(barrier, (n_gx - 1) + (n_gz - 1) + 2)

    def tell_line(i, c):
        pl.semaphore_signal(
            line_sem, inc=1, device_id={"gz": lax.rem(gz + i, n_gz)}, device_id_type=MESH
        )
        return c

    lax.fori_loop(1, n_gz, tell_line, 0)

    def zt_copy(i):
        to = lax.rem(gx + i, n_gx)
        return pltpu.make_async_remote_copy(
            src_ref=tp_v.at[to],
            dst_ref=rt_v.at[gx, gz],
            send_sem=zt_send,
            recv_sem=zt_recv,
            device_id={"gx": to},
            device_id_type=MESH,
        )

    def zt_start(i, c):
        zt_copy(i).start()
        return c

    lax.fori_loop(1, n_gx, zt_start, 0)
    rt_v[gx, gz] = tp_v[gx]

    send(face_z(0, 0) + face_z(0, 1))
    for j in range(1, layers - 1):
        start_layer(j)
        send(faces_xy(0, j - 1) if layers - 2 == PARTS else [])

    for j in range(layers):
        out = jnp.dot(sel_v[...], mean_v[j], preferred_element_type=jnp.float32)
        tx_v[pl.ds(j, groups * CAP, stride=tile), :] = out[:, :cols]
        tx_v[pl.ds(layers + j, groups * CAP, stride=tile), :] = out[:, cols:]
    rx_v[pl.ds(pl.multiple_of(me * per, 8), per), :] = tx_v[
        pl.ds(pl.multiple_of(me * per, 8), per), :
    ]
    pl.semaphore_wait(line_sem, n_gz - 1)

    def land_copy(off_gx, off_gz):
        to_gx = lax.rem(gx + off_gx, n_gx)
        to_gz = lax.rem(gz + off_gz, n_gz)
        to = to_gx * n_gz + to_gz
        pltpu.make_async_remote_copy(
            src_ref=tx_v.at[pl.ds(pl.multiple_of(to * per, 8), per), :],
            dst_ref=rx_v.at[pl.ds(pl.multiple_of(me * per, 8), per), :],
            send_sem=land_send,
            recv_sem=land_recv,
            device_id={"gx": to_gx, "gz": to_gz},
            device_id_type=MESH,
        ).start()

    n_across = n_gx * (n_gz - 1)
    n_land = groups - 1

    def land_across(i, c):
        land_copy(i // (n_gz - 1), 1 + lax.rem(i, n_gz - 1))
        return c

    def land_along(i, c):
        land_copy(1 + i - n_across, 0)
        return c

    def land_starts(begin, end):
        if begin < min(end, n_across):
            lax.fori_loop(begin, min(end, n_across), land_across, 0)
        if max(begin, n_across) < end:
            lax.fori_loop(max(begin, n_across), end, land_along, 0)

    at1 = PACE[0] * groups // 64
    at2 = at1 + PACE[1] * groups // 64
    land_starts(0, at1)

    def drain(ref, count, sem):
        pltpu.make_async_copy(ref.at[pl.ds(0, count)], ref.at[pl.ds(0, count)], sem).wait()

    drain(tp_v, n_gx - 1, zt_recv)

    def xt_copy(i):
        return pltpu.make_async_remote_copy(
            src_ref=rt_v.at[:, gz],
            dst_ref=rt_v.at[:, gz],
            send_sem=xt_send,
            recv_sem=xt_recv,
            device_id={"gz": lax.rem(gz + i, n_gz)},
            device_id_type=MESH,
        )

    for i in range(1, n_gz):
        xt_copy(i).start()
    land_starts(at1, at2)

    sign = jnp.where(jnp.bitwise_and(lane, 15) < half, 1.0, -1.0)

    def wait_part(k, part):
        views = [(2 * part + d, xh.at[k, d, part]) for d in range(2)]
        views += [(4 + 2 * part + d, yh.at[k, d, part]) for d in range(2)]
        if part == 0:
            for d, plane in enumerate((0, levels + 1)):
                for f, ref in enumerate((hp[k], kp[k])):
                    views.append((8 + 2 * f + d, ref.at[plane, pl.ds(PAD, rows), :]))
        for slot, view in views:
            pltpu.make_async_copy(view, view, h_recv.at[k * 12 + slot]).wait()

        if part == 0:
            for plane, edge, at_end in ((0, 1, 0), (levels + 1, levels, n_gz - 1)):

                @pl.when(gz == at_end)
                def _():
                    hp[k][plane, pl.ds(PAD, rows), :] = hp[k][edge, pl.ds(PAD, rows), :]
                    kp[k][plane, pl.ds(PAD, rows), :] = -kp[k][edge, pl.ds(PAD, rows), :]

        for d in range(2):

            @pl.when(role == (0 if d == 0 else n_role - 1))
            def _():
                yh[k, d, part] = ys[k, d, part] * sign

            @pl.when(gx == (0 if d == 0 else n_gx - 1))
            def _():
                xh[k, d, part, 0] = xs[k, d, part, 0]
                xh[k, d, part, 1] = -xs[k, d, part, 1]

        for d, row in ((0, PAD - 1), (1, PAD + rows)):
            for f, ref in enumerate((hp[k], kp[k])):
                for i in range(half):
                    z = level_at(part, i)
                    ref[z + 1, row : row + 1, :] = xh[k, d, part, f, i : i + 1, :]

    def stencil(k, part, at0, z, r0):
        def cut(ref, plane, shift):
            return ref[k][plane, pl.ds(PAD + r0 + shift, CHUNK), :]

        h, c = cut(hp, z + 1, 0), cut(kp, z + 1, 0)
        first, last = wide_lane == 0, wide_lane == 127
        c_ym = jnp.where(first, take_y(k, 0, part, r0, at0, 1), pltpu.roll(c, 1, 1))
        c_yp = jnp.where(last, take_y(k, 1, part, r0, at0, 1), pltpu.roll(c, 127, 1))
        h_ym = jnp.where(first, take_y(k, 0, part, r0, at0, 0), pltpu.roll(h, 1, 1))
        h_yp = jnp.where(last, take_y(k, 1, part, r0, at0, 0), pltpu.roll(h, 127, 1))
        c_up, c_dn = cut(kp, z, 0), cut(kp, z + 2, 0)
        kf_up = c + c_up
        kf_dn = c + c_dn
        kf_xm = c + cut(kp, z + 1, -1)
        kf_xp = c + cut(kp, z + 1, 1)
        kf_ym = c + c_ym
        kf_yp = c + c_yp
        flux = kf_up * (h - cut(hp, z, 0)) + kf_dn * (h - cut(hp, z + 2, 0))
        flux = flux + kf_xm * (h - cut(hp, z + 1, -1)) + kf_xp * (h - cut(hp, z + 1, 1))
        flux = flux + kf_ym * (h - h_ym) + kf_yp * (h - h_yp)
        diag = 2.0 + ((kf_up + kf_dn) + (kf_xm + kf_xp) + (kf_ym + kf_yp))
        return h, flux + (c_dn - c_up), diag

    def first_half(part, level, i, c):
        z = level(i)
        for r0 in range(0, rows, CHUNK):
            _, resid, diag = stencil(0, part, i, z, r0)
            ra_v[z, pl.ds(r0, CHUNK), :] = resid
            da_v[z, pl.ds(r0, CHUNK), :] = OMEGAS[0] / diag
        return c

    for part in range(PARTS):
        wait_part(0, part)
        for begin, end, level in segments[part]:
            lax.fori_loop(begin, end, functools.partial(first_half, part, level), 0, unroll=2)

    ref3 = rt_v.at[:, pl.ds(0, n_gz - 1)]
    pltpu.make_async_copy(ref3, ref3, xt_recv).wait()

    pieces = jnp.concatenate(split3(rt_v[...].reshape(groups * 8, cols)), axis=1)
    got = jnp.dot(get_v[...], pieces, preferred_element_type=jnp.float32)
    got = got[:, :cols] + got[:, cols : 2 * cols] + got[:, 2 * cols :]
    tq_v[...] = got[:rows]
    rq_v[...] = got[rows:] + (1.0 - act_v[...])

    def root_weight(depth, roots):
        return jnp.where(depth < roots, math.exp(-depth / 4.0), 0.0)

    for r0 in range(0, rows, CHUNK):
        rs = pl.ds(r0, CHUNK)
        roots = rq_v[rs, :]
        total = root_weight(0, roots)
        for depth in range(1, layers * n_gz):
            total = total + root_weight(depth, roots)
        scale = tq_v[rs, :]
        for j in range(layers):
            depth = (gz * layers + j).astype(jnp.float32)
            weight = jnp.where(
                depth < roots, jnp.exp(jnp.full((CHUNK, 128), -0.25, jnp.float32) * depth), 0.0
            )
            lh = lh_v[j, rs, :]
            stress = 1.0 / (1.0 + lh * lh * (1.0 / 2.25))
            sk_v[j, rs, :] = 2.0 * (scale * (weight / total) * stress)

    def curve_into(k, part, at0, z, r0, head):
        rs = pl.ds(r0, CHUNK)
        sat, cond = curves(head, la_v[z, rs, :], vn_v[z, rs, :], m_v[z, rs, :], ks_v[z, rs, :])
        put(k, part, at0, z, r0, head, cond)
        gain = po_v[z, rs, :] * sat - th_v[z, rs, :]
        ra_v[z, rs, :] = (gain + gain) + sk_v[z // LEVELS_PER_LAYER, rs, :]

    def second_half(part, level, i, c):
        z = level(i)
        for r0 in range(0, rows, CHUNK):
            rs = pl.ds(r0, CHUNK)
            resid = ra_v[z, rs, :] + sk_v[z // LEVELS_PER_LAYER, rs, :]
            head = hp[0][z + 1, pl.ds(PAD + r0, CHUNK), :]
            curve_into(1, part, i, z, r0, head - resid * da_v[z, rs, :])
        return c

    def sweep_level(k, part, level, i, c):
        z = level(i)
        for r0 in range(0, rows, CHUNK):
            rs = pl.ds(r0, CHUNK)
            head, flux, diag = stencil(k, part, i, z, r0)
            head = head - (ra_v[z, rs, :] + flux) * (OMEGAS[k] / diag)
            if k + 1 < SWEEPS:
                curve_into(k + 1, part, i, z, r0, head)
            else:
                out_p[z, rs, :] = head
        return c

    def run(k, part, body):
        for begin, end, level in segments[part]:
            lax.fori_loop(begin, end, functools.partial(body, part, level), 0, unroll=2)
            if k < SWEEPS and part == 0 and begin == 0:
                send(face_z(k, 0) + face_z(k, 1))
        if k < SWEEPS:
            send(faces_xy(k, part))

    for part in range(PARTS):
        run(1, part, second_half)
    land_starts(at2, n_land)
    for part in range(PARTS):
        wait_part(1, part)
        run(2, part, functools.partial(sweep_level, 1))

    for load in loads[8:]:
        load.wait()
    all_but_me = rx_v.at[pl.ds(0, (groups - 1) * per), :]
    pltpu.make_async_copy(all_but_me, all_but_me, land_recv).wait()
    sub = min(8, n_gx)
    n_layers = layers * n_gz
    for block in range(n_gx // sub):
        for r in range(CAP):
            b0 = block * sub

            def slots(ref, at3, stride):
                return ref[pl.ds(at3, sub, stride=stride), :]

            tpot = slots(tr_v, b0 * CAP + r, CAP)
            air = slots(ai_v, b0 * CAP + r, CAP)
            roots = slots(ro_v, b0 * CAP + r, CAP).astype(jnp.float32)
            weights = [root_weight(d, roots) for d in range(n_layers)]
            total = weights[0]
            for weight in weights[1:]:
                total = total + weight
            temps, kappa, upt = [], [], []
            for d in range(n_layers):
                bz, j = d // layers, d % layers
                base = (b0 * n_gz + bz) * per + r * tile + j
                lh = slots(rx_v, base, n_gz * per)
                ls = slots(rx_v, base + layers, n_gz * per)
                stress = 1.0 / (1.0 + lh * lh * (1.0 / 2.25))
                upt.append(0.3 * (tpot * (weights[d] / total) * stress))
                kappa.append(0.25 + 0.9 * ls)
                temps.append(slots(lt_v, (b0 * CAP + r) * n_layers + d, CAP * n_layers))
            mids = [0.5 * (kappa[d] + kappa[d + 1]) for d in range(n_layers - 1)]
            old = temps
            for _ in range(HEAT_STEPS):
                fresh = []
                for d in range(n_layers):
                    move = (
                        kappa[0] * (air - temps[0])
                        if d == 0
                        else mids[d - 1] * (temps[d - 1] - temps[d])
                    )
                    if d < n_layers - 1:
                        move = move + mids[d] * (temps[d + 1] - temps[d])
                    fresh.append(temps[d] + 0.2 * move - upt[d])
                temps = fresh
            filled = cnt_v[b0 : b0 + sub, :] > r
            for d in range(n_layers):
                out_lt[pl.ds((b0 * CAP + r) * n_layers + d, sub, stride=CAP * n_layers), :] = (
                    jnp.where(filled, temps[d], old[d])
                )

    for part in range(PARTS):
        wait_part(2, part)
        run(3, part, functools.partial(sweep_level, 2))

    for copy in started:
        copy.wait_send()
    drain(tp_v, n_gx - 1, zt_send)
    pltpu.make_async_copy(ref3, ref3, xt_send).wait()
    pltpu.make_async_copy(all_but_me, all_but_me, land_send).wait()


def solution(mesh):
    n_role, n_gx, n_gz = (mesh.shape[a] for a in ("role", "gx", "gz"))

    def local(p, al, vn, ks, po, owner, land, transp, air, roots):
        levels, rows, cols = p.shape
        layers = levels // LEVELS_PER_LAYER
        n_layers = layers * n_gz
        groups = n_gx * n_gz
        slots = n_gx * CAP
        f32 = jnp.float32
        cell = pltpu.VMEM((levels, rows, cols), f32)
        padded = pltpu.VMEM((levels + 2, rows + 2 * PAD, cols), f32)
        xface = pltpu.VMEM((SWEEPS, 2, PARTS, 2, levels // PARTS, cols), f32)
        yface = pltpu.VMEM((SWEEPS, 2, PARTS, 8, cols), f32)
        line = pltpu.VMEM((slots, cols), f32)
        payload = pltpu.VMEM((groups * CAP * 2 * layers, cols), f32)
        dma = pltpu.SemaphoreType.DMA
        head, temps = pl.pallas_call(
            functools.partial(kernel, n_role, n_gx, n_gz),
            out_shape=(
                jax.ShapeDtypeStruct(p.shape, f32),
                jax.ShapeDtypeStruct((slots * n_layers, cols), f32),
            ),
            in_specs=[pl.BlockSpec(memory_space=pl.ANY)] * 10,
            out_specs=[pl.BlockSpec(memory_space=pltpu.VMEM)] * 2,
            scratch_shapes=[
                cell,
                cell,
                cell,
                cell,
                cell,
                cell,
                cell,
                cell,
                padded,
                padded,
                padded,
                padded,
                padded,
                padded,
                xface,
                xface,
                yface,
                yface,
                pltpu.VMEM(owner.shape[::-1], jnp.int32),
                pltpu.VMEM((slots * n_layers, cols), f32),
                line,
                line,
                pltpu.VMEM((slots, cols), jnp.int32),
                pltpu.VMEM((groups * CAP, 256), jnp.bfloat16),
                pltpu.VMEM((2 * rows, groups * 8), jnp.bfloat16),
                pltpu.VMEM((rows, cols), f32),
                pltpu.VMEM((n_gx, cols), f32),
                pltpu.VMEM((n_gx, 8, cols), f32),
                pltpu.VMEM((n_gx, n_gz, 8, cols), f32),
                pltpu.VMEM((rows, cols), f32),
                pltpu.VMEM((rows, cols), f32),
                pltpu.VMEM((layers, rows, cols), f32),
                pltpu.VMEM((layers, rows, cols), f32),
                pltpu.VMEM((layers, 256, 2 * cols), jnp.bfloat16),
                payload,
                payload,
                dma((10,)),
                dma,
                dma,
                dma,
                dma,
                dma((SWEEPS * 12,)),
                dma((SWEEPS * 12,)),
                dma,
                dma,
                pltpu.SemaphoreType.REGULAR,
            ],
            compiler_params=pltpu.CompilerParams(
                collective_id=0, has_side_effects=True, vmem_limit_bytes=56 * 1024 * 1024
            ),
        )(
            p,
            al,
            vn,
            ks,
            po,
            owner.T,
            land.reshape(slots * n_layers, cols),
            transp.reshape(slots, cols),
            air.reshape(slots, cols),
            roots.reshape(slots, cols),
        )
        return head, temps.reshape(land.shape)

    grid = P("gz", "gx", "role")
    slot = P("role", ("gx", "gz"), None, None)
    return jax.shard_map(
        local,
        mesh=mesh,
        in_specs=(grid,) * 5 + (P(), P("role", ("gx", "gz"), None, None, None)) + (slot,) * 3,
        out_specs=(grid, P("role", ("gx", "gz"), None, None, None)),
        check_vma=False,
    )
```

```python
import functools
import math

import jax
import jax.numpy as jnp
from jax import lax
from jax.experimental import pallas as pl
from jax.experimental.pallas import tpu as pltpu
from jax.sharding import PartitionSpec as P

LEVELS_PER_LAYER = 4
CAP = 3
SWEEPS = 3
HEAT_STEPS = 4
LOG2E = 1.0 / math.log(2.0)
CHUNK = 32
PARTS = 2
PACE = (48, 0)
PAD = 8
MESH = pl.DeviceIdType.MESH
OMEGAS = [
    1.0 / (1.0 + 0.6 * math.cos(math.pi * (2 * k + 1) / (2 * SWEEPS))) for k in range(SWEEPS)
]


def curves(head, la, vn, m, ks):
    lx = vn * (la + (0.5 * LOG2E) * jnp.log(head * head + 0.01))
    soft = jnp.log(1.0 + jnp.exp2(lx)) * LOG2E
    root = jnp.exp2(-0.5 * (m * soft))
    gap = 1.0 - jnp.exp2(m * (lx - soft))
    return root * root, ks * root * (gap * gap)


def split3(x):
    hi = x.astype(jnp.bfloat16)
    rest = x - hi.astype(jnp.float32)
    mid = rest.astype(jnp.bfloat16)
    return hi, mid, (rest - mid.astype(jnp.float32)).astype(jnp.bfloat16)


def kernel(
    n_role,
    n_gx,
    n_gz,
    p_hbm,
    al_hbm,
    vn_hbm,
    ks_hbm,
    po_hbm,
    own_hbm,
    lt_hbm,
    tr_hbm,
    ai_hbm,
    ro_hbm,
    out_p,
    out_lt,
    la_v,
    vn_v,
    ks_v,
    po_v,
    m_v,
    th_v,
    ra_v,
    da_v,
    hp0,
    hp1,
    hp2,
    kp0,
    kp1,
    kp2,
    xs,
    xh,
    ys,
    yh,
    own_v,
    lt_v,
    tr_v,
    ai_v,
    ro_v,
    sel_v,
    get_v,
    act_v,
    cnt_v,
    tp_v,
    rt_v,
    tq_v,
    rq_v,
    sk_v,
    lh_v,
    mean_v,
    tx_v,
    rx_v,
    load_sem,
    zt_send,
    zt_recv,
    xt_send,
    xt_recv,
    h_send,
    h_recv,
    land_send,
    land_recv,
    line_sem,
):
    levels, rows, cols = p_hbm.shape
    layers = levels // LEVELS_PER_LAYER
    groups = n_gx * n_gz
    tile = 2 * layers
    per = CAP * tile
    role = lax.axis_index("role")
    gx = lax.axis_index("gx")
    gz = lax.axis_index("gz")
    me = gx * n_gz + gz
    hp = (hp0, hp1, hp2)
    kp = (kp0, kp1, kp2)
    half = levels // PARTS

    barrier = pltpu.get_barrier_semaphore()

    def greet_gx(i, c):
        pl.semaphore_signal(
            barrier, inc=1, device_id={"gx": lax.rem(gx + i, n_gx)}, device_id_type=MESH
        )
        return c

    def greet_gz(i, c):
        pl.semaphore_signal(
            barrier, inc=1, device_id={"gz": lax.rem(gz + i, n_gz)}, device_id_type=MESH
        )
        return c

    lax.fori_loop(1, n_gx, greet_gx, 0)
    lax.fori_loop(1, n_gz, greet_gz, 0)
    for step in (1, n_role - 1):
        pl.semaphore_signal(
            barrier, inc=1, device_id={"role": lax.rem(role + step, n_role)}, device_id_type=MESH
        )

    pairs = (
        (tr_hbm, tr_v),
        (ro_hbm, ro_v),
        (own_hbm, own_v),
        (p_hbm, hp0.at[pl.ds(1, levels), pl.ds(PAD, rows), :]),
        (al_hbm, la_v),
        (vn_hbm, vn_v),
        (ks_hbm, ks_v),
        (po_hbm, po_v),
        (lt_hbm, lt_v),
        (ai_hbm, ai_v),
    )
    loads = [pltpu.make_async_copy(a, b, load_sem.at[i]) for i, (a, b) in enumerate(pairs)]
    for load in loads:
        load.start()

    loads[0].wait()
    loads[1].wait()
    for b in range(n_gx):
        tp_v[b, CAP:4, :] = jnp.zeros((1, cols), jnp.float32)
        tp_v[b, 4 + CAP :, :] = jnp.zeros((1, cols), jnp.float32)
        tp_v[b, 0:CAP, :] = tr_v[b * CAP : (b + 1) * CAP, :]
        tp_v[b, 4 : 4 + CAP, :] = ro_v[b * CAP : (b + 1) * CAP, :].astype(jnp.float32)

    loads[2].wait()
    lane1 = lax.broadcasted_iota(jnp.int32, (1, 128), 1)
    sub4 = lax.broadcasted_iota(jnp.int32, (n_role, 128), 0)

    def role_lanes(start):
        return jnp.sum(
            jnp.where(sub4 == role, own_v[:, pl.ds(start, 128)], 0), axis=0, keepdims=True
        )

    pair = role_lanes(pl.multiple_of((gx // 2) * 128, 128))
    own = jnp.where(lax.rem(gx, 2) == 1, pltpu.roll(pair, 64, 1), pair)
    ii = lax.broadcasted_iota(jnp.int32, (128, 128), 0)
    jj = lax.broadcasted_iota(jnp.int32, (128, 128), 1)
    by_lane = jnp.broadcast_to(own, (128, 128))
    by_sub = jnp.transpose(by_lane)
    earlier = (by_lane == by_sub) & (ii < jj) & (ii < rows)
    rank_lane = jnp.sum(jnp.where(earlier, 1, 0), axis=0, keepdims=True)
    rank_sub = jnp.transpose(jnp.broadcast_to(rank_lane, (128, 128)))
    key = jnp.where((own >= 0) & (lane1 < rows), own * CAP + rank_lane + 1, 0)
    key = jnp.broadcast_to(key + pltpu.roll(key, 64, 1), (groups * CAP, 128))
    slot = lax.broadcasted_iota(jnp.int32, (groups * CAP, 128), 0) + 1
    wide = lax.broadcasted_iota(jnp.int32, (groups * CAP, 128), 1)
    pick = key == slot
    sel_v[:, 0:128] = jnp.where(pick, 1.0, 0.0).astype(jnp.bfloat16)
    sel_v[:, 128:256] = jnp.where(pick & (wide < rows), 1.0, 0.0).astype(jnp.bfloat16)
    at = jnp.where(by_sub >= 0, by_sub * 8 + rank_sub, -8)[:rows]
    width = min(128, groups * 8)
    for t in range(groups * 8 // width):
        for f in range(2):
            hit = at + 4 * f == jj[:rows] + t * width
            get_v[f * rows : (f + 1) * rows, t * width : (t + 1) * width] = jnp.where(
                hit[:, :width], 1.0, 0.0
            ).astype(jnp.bfloat16)
    act_v[...] = jnp.where(by_sub[:rows] >= 0, 1.0, 0.0)
    for t in range(n_gx // 2):
        hit = jnp.where(role_lanes(t * 128) == me, 1.0, 0.0)
        for side in range(2):
            part = jnp.where((lane1 < 64) == (side == 0), hit, 0.0)
            cnt_v[2 * t + side : 2 * t + side + 1, :] = jnp.broadcast_to(
                jnp.sum(part, axis=1, keepdims=True), (1, 128)
            )

    segments = (
        ((0, 2, lambda i: i * (levels - 1)), (2, half, lambda i: i - 1)),
        ((0, half, lambda i: half - 1 + i),),
    )

    def level_at(part, i):
        return next(at(i) for begin, end, at in segments[part] if begin <= i < end)

    def place_of(z):
        if z in (0, levels - 1):
            return 0, min(z, 1)
        return (0, z + 1) if z < half - 1 else (1, z - half + 1)

    lane = lax.broadcasted_iota(jnp.int32, (8, 128), 1)
    wide_lane = lax.broadcasted_iota(jnp.int32, (CHUNK, 128), 1)

    def pack_y(k, d, part, r0, at0, head, cond):
        face = ys[k, d, part]
        for g in range(r0 // 8, (r0 + CHUNK) // 8):
            for f, ref in enumerate((head, cond)):
                to = g * 16 + f * half + at0
                shift = to if d == 0 else jnp.bitwise_and(to + 1, 127)
                face = jnp.where(
                    lane == to, pltpu.roll(ref[g * 8 - r0 : g * 8 - r0 + 8], shift, 1), face
                )
        ys[k, d, part] = face

    def take_y(k, d, part, r0, at0, f):
        face = yh[k, d, part]
        end = 128 if d == 0 else 127
        return jnp.concatenate(
            [
                pltpu.roll(face, end - g * 16 - f * half - at0, 1)
                for g in range(r0 // 8, (r0 + CHUNK) // 8)
            ],
            axis=0,
        )

    def put(k, part, at0, z, r0, head, cond, keep_head=True):
        if keep_head:
            hp[k][z + 1, pl.ds(PAD + r0, CHUNK), :] = head
        kp[k][z + 1, pl.ds(PAD + r0, CHUNK), :] = cond
        if r0 == 0:
            xs[k, 0, part, 0, pl.ds(at0, 1), :] = head[0:1]
            xs[k, 0, part, 1, pl.ds(at0, 1), :] = cond[0:1]
        if r0 + CHUNK == rows:
            xs[k, 1, part, 0, pl.ds(at0, 1), :] = head[CHUNK - 1 :]
            xs[k, 1, part, 1, pl.ds(at0, 1), :] = cond[CHUNK - 1 :]
        for d in range(2):
            pack_y(k, d, part, r0, at0, head, cond)

    def remote(src, dst, k, slot, dst_slot, where):
        return pltpu.make_async_remote_copy(
            src_ref=src,
            dst_ref=dst,
            send_sem=h_send.at[k * 12 + slot],
            recv_sem=h_recv.at[k * 12 + dst_slot],
            device_id=where,
            device_id_type=MESH,
        )

    started = []

    def send(copies):
        for copy in copies:
            copy.start()
        started.extend(copies)

    def face_z(k, d):
        to = lax.rem(gz + (n_gz - 1 if d == 0 else 1), n_gz)
        made = []
        for f, ref in enumerate((hp[k], kp[k])):
            src = ref.at[1 if d == 0 else levels, pl.ds(PAD, rows), :]
            dst = ref.at[levels + 1 if d == 0 else 0, pl.ds(PAD, rows), :]
            made.append(remote(src, dst, k, 8 + 2 * f + d, 8 + 2 * f + 1 - d, {"gz": to}))
        return made

    def faces_xy(k, part):
        made = []
        for d in range(2):
            to = lax.rem(gx + (n_gx - 1 if d == 0 else 1), n_gx)
            made.append(
                remote(
                    xs.at[k, d, part],
                    xh.at[k, 1 - d, part],
                    k,
                    2 * part + d,
                    2 * part + 1 - d,
                    {"gx": to},
                )
            )
        for d in range(2):
            to = lax.rem(role + (n_role - 1 if d == 0 else 1), n_role)
            made.append(
                remote(
                    ys.at[k, d, part],
                    yh.at[k, 1 - d, part],
                    k,
                    4 + 2 * part + d,
                    4 + 2 * part + 1 - d,
                    {"role": to},
                )
            )
        return made

    mean_v[:, CAP * rows :, :] = jnp.zeros((layers, 256 - CAP * rows, 2 * cols), jnp.bfloat16)
    for load in loads[3:8]:
        load.wait()

    def start_layer(j):
        for r0 in range(0, rows, CHUNK):
            rs = pl.ds(r0, CHUNK)
            sum_s = None
            sum_h = None
            for i in range(LEVELS_PER_LAYER):
                z = j * LEVELS_PER_LAYER + i
                head = hp[0][z + 1, pl.ds(PAD + r0, CHUNK), :]
                vn = vn_v[z, rs, :]
                la = jnp.log(la_v[z, rs, :]) * LOG2E
                m = 1.0 - 1.0 / vn
                la_v[z, rs, :] = la
                m_v[z, rs, :] = m
                sat, cond = curves(head, la, vn, m, ks_v[z, rs, :])
                th_v[z, rs, :] = po_v[z, rs, :] * sat
                part, at0 = place_of(z)
                put(0, part, at0, z, r0, head, cond, keep_head=False)
                sum_s = sat if sum_s is None else sum_s + sat
                sum_h = head if sum_h is None else sum_h + head
            mean_h = sum_h * 0.25
            lh_v[j, rs, :] = mean_h
            for f, mean in enumerate((mean_h, sum_s * 0.25)):
                for piece, value in enumerate(split3(mean)):
                    mean_v[
                        j,
                        piece * rows + r0 : piece * rows + r0 + CHUNK,
                        f * cols : (f + 1) * cols,
                    ] = value

    start_layer(0)
    start_layer(layers - 1)

    for j in range(1, layers - 1):
        start_layer(j)

    for j in range(layers):
        out = jnp.dot(sel_v[...], mean_v[j], preferred_element_type=jnp.float32)
        tx_v[pl.ds(j, groups * CAP, stride=tile), :] = out[:, :cols]
        tx_v[pl.ds(layers + j, groups * CAP, stride=tile), :] = out[:, cols:]
    rx_v[pl.ds(pl.multiple_of(me * per, 8), per), :] = tx_v[
        pl.ds(pl.multiple_of(me * per, 8), per), :
    ]
    pl.semaphore_wait(barrier, (n_gx - 1) + (n_gz - 1) + 2)

    def tell_line(i, c):
        pl.semaphore_signal(
            line_sem, inc=1, device_id={"gz": lax.rem(gz + i, n_gz)}, device_id_type=MESH
        )
        return c

    lax.fori_loop(1, n_gz, tell_line, 0)

    def zt_copy(i):
        to = lax.rem(gx + i, n_gx)
        return pltpu.make_async_remote_copy(
            src_ref=tp_v.at[to],
            dst_ref=rt_v.at[gx, gz],
            send_sem=zt_send,
            recv_sem=zt_recv,
            device_id={"gx": to},
            device_id_type=MESH,
        )

    def zt_start(i, c):
        zt_copy(i).start()
        return c

    lax.fori_loop(1, n_gx, zt_start, 0)
    rt_v[gx, gz] = tp_v[gx]

    send(face_z(0, 0) + face_z(0, 1))
    for part in range(PARTS):
        send(faces_xy(0, part))

    pl.semaphore_wait(line_sem, n_gz - 1)

    def land_copy(off_gx, off_gz):
        to_gx = lax.rem(gx + off_gx, n_gx)
        to_gz = lax.rem(gz + off_gz, n_gz)
        to = to_gx * n_gz + to_gz
        pltpu.make_async_remote_copy(
            src_ref=tx_v.at[pl.ds(pl.multiple_of(to * per, 8), per), :],
            dst_ref=rx_v.at[pl.ds(pl.multiple_of(me * per, 8), per), :],
            send_sem=land_send,
            recv_sem=land_recv,
            device_id={"gx": to_gx, "gz": to_gz},
            device_id_type=MESH,
        ).start()

    n_across = n_gx * (n_gz - 1)
    n_land = groups - 1

    def land_across(i, c):
        land_copy(i // (n_gz - 1), 1 + lax.rem(i, n_gz - 1))
        return c

    def land_along(i, c):
        land_copy(1 + i - n_across, 0)
        return c

    def land_starts(begin, end):
        if begin < min(end, n_across):
            lax.fori_loop(begin, min(end, n_across), land_across, 0)
        if max(begin, n_across) < end:
            lax.fori_loop(max(begin, n_across), end, land_along, 0)

    at1 = PACE[0] * groups // 64
    at2 = at1 + PACE[1] * groups // 64
    land_starts(0, at1)

    def drain(ref, count, sem):
        pltpu.make_async_copy(ref.at[pl.ds(0, count)], ref.at[pl.ds(0, count)], sem).wait()

    drain(tp_v, n_gx - 1, zt_recv)

    def xt_copy(i):
        return pltpu.make_async_remote_copy(
            src_ref=rt_v.at[:, gz],
            dst_ref=rt_v.at[:, gz],
            send_sem=xt_send,
            recv_sem=xt_recv,
            device_id={"gz": lax.rem(gz + i, n_gz)},
            device_id_type=MESH,
        )

    for i in range(1, n_gz):
        xt_copy(i).start()
    land_starts(at1, at2)

    sign = jnp.where(jnp.bitwise_and(lane, 15) < half, 1.0, -1.0)

    def wait_part(k, part):
        views = [(2 * part + d, xh.at[k, d, part]) for d in range(2)]
        views += [(4 + 2 * part + d, yh.at[k, d, part]) for d in range(2)]
        if part == 0:
            for d, plane in enumerate((0, levels + 1)):
                for f, ref in enumerate((hp[k], kp[k])):
                    views.append((8 + 2 * f + d, ref.at[plane, pl.ds(PAD, rows), :]))
        for slot, view in views:
            pltpu.make_async_copy(view, view, h_recv.at[k * 12 + slot]).wait()

        if part == 0:
            for plane, edge, at_end in ((0, 1, 0), (levels + 1, levels, n_gz - 1)):

                @pl.when(gz == at_end)
                def _():
                    hp[k][plane, pl.ds(PAD, rows), :] = hp[k][edge, pl.ds(PAD, rows), :]
                    kp[k][plane, pl.ds(PAD, rows), :] = -kp[k][edge, pl.ds(PAD, rows), :]

        for d in range(2):

            @pl.when(role == (0 if d == 0 else n_role - 1))
            def _():
                yh[k, d, part] = ys[k, d, part] * sign

            @pl.when(gx == (0 if d == 0 else n_gx - 1))
            def _():
                xh[k, d, part, 0] = xs[k, d, part, 0]
                xh[k, d, part, 1] = -xs[k, d, part, 1]

        for d, row in ((0, PAD - 1), (1, PAD + rows)):
            for f, ref in enumerate((hp[k], kp[k])):
                for i in range(half):
                    z = level_at(part, i)
                    ref[z + 1, row : row + 1, :] = xh[k, d, part, f, i : i + 1, :]

    def stencil(k, part, at0, z, r0):
        def cut(ref, plane, shift):
            return ref[k][plane, pl.ds(PAD + r0 + shift, CHUNK), :]

        h, c = cut(hp, z + 1, 0), cut(kp, z + 1, 0)
        first, last = wide_lane == 0, wide_lane == 127
        c_ym = jnp.where(first, take_y(k, 0, part, r0, at0, 1), pltpu.roll(c, 1, 1))
        c_yp = jnp.where(last, take_y(k, 1, part, r0, at0, 1), pltpu.roll(c, 127, 1))
        h_ym = jnp.where(first, take_y(k, 0, part, r0, at0, 0), pltpu.roll(h, 1, 1))
        h_yp = jnp.where(last, take_y(k, 1, part, r0, at0, 0), pltpu.roll(h, 127, 1))
        c_up, c_dn = cut(kp, z, 0), cut(kp, z + 2, 0)
        kf_up = c + c_up
        kf_dn = c + c_dn
        kf_xm = c + cut(kp, z + 1, -1)
        kf_xp = c + cut(kp, z + 1, 1)
        kf_ym = c + c_ym
        kf_yp = c + c_yp
        flux = kf_up * (h - cut(hp, z, 0)) + kf_dn * (h - cut(hp, z + 2, 0))
        flux = flux + kf_xm * (h - cut(hp, z + 1, -1)) + kf_xp * (h - cut(hp, z + 1, 1))
        flux = flux + kf_ym * (h - h_ym) + kf_yp * (h - h_yp)
        diag = 2.0 + ((kf_up + kf_dn) + (kf_xm + kf_xp) + (kf_ym + kf_yp))
        return h, flux + (c_dn - c_up), diag

    def first_half(part, level, i, c):
        z = level(i)
        for r0 in range(0, rows, CHUNK):
            _, resid, diag = stencil(0, part, i, z, r0)
            ra_v[z, pl.ds(r0, CHUNK), :] = resid
            da_v[z, pl.ds(r0, CHUNK), :] = OMEGAS[0] / diag
        return c

    for part in range(PARTS):
        wait_part(0, part)
        for begin, end, level in segments[part]:
            lax.fori_loop(begin, end, functools.partial(first_half, part, level), 0, unroll=2)

    ref3 = rt_v.at[:, pl.ds(0, n_gz - 1)]
    pltpu.make_async_copy(ref3, ref3, xt_recv).wait()

    pieces = jnp.concatenate(split3(rt_v[...].reshape(groups * 8, cols)), axis=1)
    got = jnp.dot(get_v[...], pieces, preferred_element_type=jnp.float32)
    got = got[:, :cols] + got[:, cols : 2 * cols] + got[:, 2 * cols :]
    tq_v[...] = got[:rows]
    rq_v[...] = got[rows:] + (1.0 - act_v[...])

    def root_weight(depth, roots):
        return jnp.where(depth < roots, math.exp(-depth / 4.0), 0.0)

    for r0 in range(0, rows, CHUNK):
        rs = pl.ds(r0, CHUNK)
        roots = rq_v[rs, :]
        total = root_weight(0, roots)
        for depth in range(1, layers * n_gz):
            total = total + root_weight(depth, roots)
        scale = tq_v[rs, :]
        for j in range(layers):
            depth = (gz * layers + j).astype(jnp.float32)
            weight = jnp.where(
                depth < roots, jnp.exp(jnp.full((CHUNK, 128), -0.25, jnp.float32) * depth), 0.0
            )
            lh = lh_v[j, rs, :]
            stress = 1.0 / (1.0 + lh * lh * (1.0 / 2.25))
            sk_v[j, rs, :] = 2.0 * (scale * (weight / total) * stress)

    def curve_into(k, part, at0, z, r0, head):
        rs = pl.ds(r0, CHUNK)
        sat, cond = curves(head, la_v[z, rs, :], vn_v[z, rs, :], m_v[z, rs, :], ks_v[z, rs, :])
        put(k, part, at0, z, r0, head, cond)
        gain = po_v[z, rs, :] * sat - th_v[z, rs, :]
        ra_v[z, rs, :] = (gain + gain) + sk_v[z // LEVELS_PER_LAYER, rs, :]

    def second_half(part, level, i, c):
        z = level(i)
        for r0 in range(0, rows, CHUNK):
            rs = pl.ds(r0, CHUNK)
            resid = ra_v[z, rs, :] + sk_v[z // LEVELS_PER_LAYER, rs, :]
            head = hp[0][z + 1, pl.ds(PAD + r0, CHUNK), :]
            curve_into(1, part, i, z, r0, head - resid * da_v[z, rs, :])
        return c

    def sweep_level(k, part, level, i, c):
        z = level(i)
        for r0 in range(0, rows, CHUNK):
            rs = pl.ds(r0, CHUNK)
            head, flux, diag = stencil(k, part, i, z, r0)
            head = head - (ra_v[z, rs, :] + flux) * (OMEGAS[k] / diag)
            if k + 1 < SWEEPS:
                curve_into(k + 1, part, i, z, r0, head)
            else:
                out_p[z, rs, :] = head
        return c

    def run(k, part, body):
        for begin, end, level in segments[part]:
            lax.fori_loop(begin, end, functools.partial(body, part, level), 0, unroll=2)
            if k < SWEEPS and part == 0 and begin == 0:
                send(face_z(k, 0) + face_z(k, 1))
        if k < SWEEPS:
            send(faces_xy(k, part))

    for part in range(PARTS):
        run(1, part, second_half)
    land_starts(at2, n_land)
    for part in range(PARTS):
        wait_part(1, part)
        run(2, part, functools.partial(sweep_level, 1))

    for load in loads[8:]:
        load.wait()
    all_but_me = rx_v.at[pl.ds(0, (groups - 1) * per), :]
    pltpu.make_async_copy(all_but_me, all_but_me, land_recv).wait()
    sub = min(8, n_gx)
    n_layers = layers * n_gz
    for block in range(n_gx // sub):
        for r in range(CAP):
            b0 = block * sub

            def slots(ref, at3, stride):
                return ref[pl.ds(at3, sub, stride=stride), :]

            tpot = slots(tr_v, b0 * CAP + r, CAP)
            air = slots(ai_v, b0 * CAP + r, CAP)
            roots = slots(ro_v, b0 * CAP + r, CAP).astype(jnp.float32)
            weights = [root_weight(d, roots) for d in range(n_layers)]
            total = weights[0]
            for weight in weights[1:]:
                total = total + weight
            temps, kappa, upt = [], [], []
            for d in range(n_layers):
                bz, j = d // layers, d % layers
                base = (b0 * n_gz + bz) * per + r * tile + j
                lh = slots(rx_v, base, n_gz * per)
                ls = slots(rx_v, base + layers, n_gz * per)
                stress = 1.0 / (1.0 + lh * lh * (1.0 / 2.25))
                upt.append(0.3 * (tpot * (weights[d] / total) * stress))
                kappa.append(0.25 + 0.9 * ls)
                temps.append(slots(lt_v, (b0 * CAP + r) * n_layers + d, CAP * n_layers))
            mids = [0.5 * (kappa[d] + kappa[d + 1]) for d in range(n_layers - 1)]
            old = temps
            for _ in range(HEAT_STEPS):
                fresh = []
                for d in range(n_layers):
                    move = (
                        kappa[0] * (air - temps[0])
                        if d == 0
                        else mids[d - 1] * (temps[d - 1] - temps[d])
                    )
                    if d < n_layers - 1:
                        move = move + mids[d] * (temps[d + 1] - temps[d])
                    fresh.append(temps[d] + 0.2 * move - upt[d])
                temps = fresh
            filled = cnt_v[b0 : b0 + sub, :] > r
            for d in range(n_layers):
                out_lt[pl.ds((b0 * CAP + r) * n_layers + d, sub, stride=CAP * n_layers), :] = (
                    jnp.where(filled, temps[d], old[d])
                )

    for part in range(PARTS):
        wait_part(2, part)
        run(3, part, functools.partial(sweep_level, 2))

    for copy in started:
        copy.wait_send()
    drain(tp_v, n_gx - 1, zt_send)
    pltpu.make_async_copy(ref3, ref3, xt_send).wait()
    pltpu.make_async_copy(all_but_me, all_but_me, land_send).wait()


def solution(mesh):
    n_role, n_gx, n_gz = (mesh.shape[a] for a in ("role", "gx", "gz"))

    def local(p, al, vn, ks, po, owner, land, transp, air, roots):
        levels, rows, cols = p.shape
        layers = levels // LEVELS_PER_LAYER
        n_layers = layers * n_gz
        groups = n_gx * n_gz
        slots = n_gx * CAP
        f32 = jnp.float32
        cell = pltpu.VMEM((levels, rows, cols), f32)
        padded = pltpu.VMEM((levels + 2, rows + 2 * PAD, cols), f32)
        xface = pltpu.VMEM((SWEEPS, 2, PARTS, 2, levels // PARTS, cols), f32)
        yface = pltpu.VMEM((SWEEPS, 2, PARTS, 8, cols), f32)
        line = pltpu.VMEM((slots, cols), f32)
        payload = pltpu.VMEM((groups * CAP * 2 * layers, cols), f32)
        dma = pltpu.SemaphoreType.DMA
        head, temps = pl.pallas_call(
            functools.partial(kernel, n_role, n_gx, n_gz),
            out_shape=(
                jax.ShapeDtypeStruct(p.shape, f32),
                jax.ShapeDtypeStruct((slots * n_layers, cols), f32),
            ),
            in_specs=[pl.BlockSpec(memory_space=pltpu.HBM)] * 10,
            out_specs=[pl.BlockSpec(memory_space=pltpu.VMEM)] * 2,
            scratch_shapes=[
                cell,
                cell,
                cell,
                cell,
                cell,
                cell,
                cell,
                cell,
                padded,
                padded,
                padded,
                padded,
                padded,
                padded,
                xface,
                xface,
                yface,
                yface,
                pltpu.VMEM(owner.shape[::-1], jnp.int32),
                pltpu.VMEM((slots * n_layers, cols), f32),
                line,
                line,
                pltpu.VMEM((slots, cols), jnp.int32),
                pltpu.VMEM((groups * CAP, 256), jnp.bfloat16),
                pltpu.VMEM((2 * rows, groups * 8), jnp.bfloat16),
                pltpu.VMEM((rows, cols), f32),
                pltpu.VMEM((n_gx, cols), f32),
                pltpu.VMEM((n_gx, 8, cols), f32),
                pltpu.VMEM((n_gx, n_gz, 8, cols), f32),
                pltpu.VMEM((rows, cols), f32),
                pltpu.VMEM((rows, cols), f32),
                pltpu.VMEM((layers, rows, cols), f32),
                pltpu.VMEM((layers, rows, cols), f32),
                pltpu.VMEM((layers, 256, 2 * cols), jnp.bfloat16),
                payload,
                payload,
                dma((10,)),
                dma,
                dma,
                dma,
                dma,
                dma((SWEEPS * 12,)),
                dma((SWEEPS * 12,)),
                dma,
                dma,
                pltpu.SemaphoreType.REGULAR,
            ],
            compiler_params=pltpu.CompilerParams(
                collective_id=0, has_side_effects=True, vmem_limit_bytes=28 * 1024 * 1024
            ),
        )(
            *[
                pltpu.with_memory_space_constraint(x, pltpu.HBM)
                for x in (
                    p,
                    al,
                    vn,
                    ks,
                    po,
                    owner.T,
                    land.reshape(slots * n_layers, cols),
                    transp.reshape(slots, cols),
                    air.reshape(slots, cols),
                    roots.reshape(slots, cols),
                )
            ]
        )
        return head, temps.reshape(land.shape)

    grid = P("gz", "gx", "role")
    slot = P("role", ("gx", "gz"), None, None)
    return jax.shard_map(
        local,
        mesh=mesh,
        in_specs=(grid,) * 5 + (P(), P("role", ("gx", "gz"), None, None, None)) + (slot,) * 3,
        out_specs=(grid, P("role", ("gx", "gz"), None, None, None)),
        check_vma=False,
    )
```

```python
import functools
import math

import jax
import jax.numpy as jnp
from jax import lax
from jax.experimental import pallas as pl
from jax.experimental.pallas import tpu as pltpu
from jax.sharding import PartitionSpec as P

LEVELS_PER_LAYER = 4
CAP = 3
SWEEPS = 3
HEAT_STEPS = 4
LOG2E = 1.0 / math.log(2.0)
CHUNK = 32
PARTS = 2
PACE = (48, 0)
PAD = 8
MESH = pl.DeviceIdType.MESH
OMEGAS = [
    1.0 / (1.0 + 0.6 * math.cos(math.pi * (2 * k + 1) / (2 * SWEEPS))) for k in range(SWEEPS)
]


def curves(head, la, vn, m, ks):
    lx = vn * (la + (0.5 * LOG2E) * jnp.log(head * head + 0.01))
    soft = jnp.log(1.0 + jnp.exp2(lx)) * LOG2E
    root = jnp.exp2(-0.5 * (m * soft))
    gap = 1.0 - jnp.exp2(m * (lx - soft))
    return root * root, ks * root * (gap * gap)


def split3(x):
    hi = x.astype(jnp.bfloat16)
    rest = x - hi.astype(jnp.float32)
    mid = rest.astype(jnp.bfloat16)
    return hi, mid, (rest - mid.astype(jnp.float32)).astype(jnp.bfloat16)


def kernel(
    n_role,
    n_gx,
    n_gz,
    p_hbm,
    al_hbm,
    vn_hbm,
    ks_hbm,
    po_hbm,
    own_hbm,
    lt_hbm,
    tr_hbm,
    ai_hbm,
    ro_hbm,
    out_p,
    out_lt,
    la_v,
    vn_v,
    ks_v,
    po_v,
    m_v,
    th_v,
    ra_v,
    da_v,
    hp0,
    hp1,
    hp2,
    kp0,
    kp1,
    kp2,
    xs,
    xh,
    ys,
    yh,
    own_v,
    lt_v,
    tr_v,
    ai_v,
    ro_v,
    sel_v,
    get_v,
    act_v,
    cnt_v,
    tp_v,
    rt_v,
    tq_v,
    rq_v,
    sk_v,
    lh_v,
    mean_v,
    tx_v,
    rx_v,
    load_sem,
    zt_send,
    zt_recv,
    xt_send,
    xt_recv,
    h_send,
    h_recv,
    land_send,
    land_recv,
    line_sem,
):
    levels, rows, cols = p_hbm.shape
    layers = levels // LEVELS_PER_LAYER
    groups = n_gx * n_gz
    tile = 2 * layers
    per = CAP * tile
    role = lax.axis_index("role")
    gx = lax.axis_index("gx")
    gz = lax.axis_index("gz")
    me = gx * n_gz + gz
    hp = (hp0, hp1, hp2)
    kp = (kp0, kp1, kp2)
    half = levels // PARTS

    pairs = (
        (tr_hbm, tr_v),
        (ro_hbm, ro_v),
        (own_hbm, own_v),
        (p_hbm, hp0.at[pl.ds(1, levels), pl.ds(PAD, rows), :]),
        (al_hbm, la_v),
        (vn_hbm, vn_v),
        (ks_hbm, ks_v),
        (po_hbm, po_v),
        (lt_hbm, lt_v),
        (ai_hbm, ai_v),
    )
    loads = [pltpu.make_async_copy(a, b, load_sem.at[i]) for i, (a, b) in enumerate(pairs)]
    for load in loads:
        load.start()

    barrier = pltpu.get_barrier_semaphore()

    def greet_gx(i, c):
        pl.semaphore_signal(
            barrier, inc=1, device_id={"gx": lax.rem(gx + i, n_gx)}, device_id_type=MESH
        )
        return c

    def greet_gz(i, c):
        pl.semaphore_signal(
            barrier, inc=1, device_id={"gz": lax.rem(gz + i, n_gz)}, device_id_type=MESH
        )
        return c

    lax.fori_loop(1, n_gx, greet_gx, 0)
    lax.fori_loop(1, n_gz, greet_gz, 0)
    for step in (1, n_role - 1):
        pl.semaphore_signal(
            barrier, inc=1, device_id={"role": lax.rem(role + step, n_role)}, device_id_type=MESH
        )

    loads[0].wait()
    loads[1].wait()
    for b in range(n_gx):
        tp_v[b, CAP:4, :] = jnp.zeros((1, cols), jnp.float32)
        tp_v[b, 4 + CAP :, :] = jnp.zeros((1, cols), jnp.float32)
        tp_v[b, 0:CAP, :] = tr_v[b * CAP : (b + 1) * CAP, :]
        tp_v[b, 4 : 4 + CAP, :] = ro_v[b * CAP : (b + 1) * CAP, :].astype(jnp.float32)

    loads[2].wait()
    lane1 = lax.broadcasted_iota(jnp.int32, (1, 128), 1)
    sub4 = lax.broadcasted_iota(jnp.int32, (n_role, 128), 0)

    def role_lanes(start):
        return jnp.sum(
            jnp.where(sub4 == role, own_v[:, pl.ds(start, 128)], 0), axis=0, keepdims=True
        )

    pair = role_lanes(pl.multiple_of((gx // 2) * 128, 128))
    own = jnp.where(lax.rem(gx, 2) == 1, pltpu.roll(pair, 64, 1), pair)
    ii = lax.broadcasted_iota(jnp.int32, (128, 128), 0)
    jj = lax.broadcasted_iota(jnp.int32, (128, 128), 1)
    by_lane = jnp.broadcast_to(own, (128, 128))
    by_sub = jnp.transpose(by_lane)
    earlier = (by_lane == by_sub) & (ii < jj) & (ii < rows)
    rank_lane = jnp.sum(jnp.where(earlier, 1, 0), axis=0, keepdims=True)
    rank_sub = jnp.transpose(jnp.broadcast_to(rank_lane, (128, 128)))
    key = jnp.where((own >= 0) & (lane1 < rows), own * CAP + rank_lane + 1, 0)
    key = jnp.broadcast_to(key + pltpu.roll(key, 64, 1), (groups * CAP, 128))
    slot = lax.broadcasted_iota(jnp.int32, (groups * CAP, 128), 0) + 1
    wide = lax.broadcasted_iota(jnp.int32, (groups * CAP, 128), 1)
    pick = key == slot
    sel_v[:, 0:128] = jnp.where(pick, 1.0, 0.0).astype(jnp.bfloat16)
    sel_v[:, 128:256] = jnp.where(pick & (wide < rows), 1.0, 0.0).astype(jnp.bfloat16)
    at = jnp.where(by_sub >= 0, by_sub * 8 + rank_sub, -8)[:rows]
    width = min(128, groups * 8)
    for t in range(groups * 8 // width):
        for f in range(2):
            hit = at + 4 * f == jj[:rows] + t * width
            get_v[f * rows : (f + 1) * rows, t * width : (t + 1) * width] = jnp.where(
                hit[:, :width], 1.0, 0.0
            ).astype(jnp.bfloat16)
    act_v[...] = jnp.where(by_sub[:rows] >= 0, 1.0, 0.0)
    for t in range(n_gx // 2):
        hit = jnp.where(role_lanes(t * 128) == me, 1.0, 0.0)
        for side in range(2):
            part = jnp.where((lane1 < 64) == (side == 0), hit, 0.0)
            cnt_v[2 * t + side : 2 * t + side + 1, :] = jnp.broadcast_to(
                jnp.sum(part, axis=1, keepdims=True), (1, 128)
            )

    segments = (
        ((0, 2, lambda i: i * (levels - 1)), (2, half, lambda i: i - 1)),
        ((0, half, lambda i: half - 1 + i),),
    )

    def level_at(part, i):
        return next(at(i) for begin, end, at in segments[part] if begin <= i < end)

    def place_of(z):
        if z in (0, levels - 1):
            return 0, min(z, 1)
        return (0, z + 1) if z < half - 1 else (1, z - half + 1)

    lane = lax.broadcasted_iota(jnp.int32, (8, 128), 1)
    wide_lane = lax.broadcasted_iota(jnp.int32, (CHUNK, 128), 1)

    def pack_y(k, d, part, r0, at0, head, cond):
        face = ys[k, d, part]
        for g in range(r0 // 8, (r0 + CHUNK) // 8):
            for f, ref in enumerate((head, cond)):
                to = g * 16 + f * half + at0
                shift = to if d == 0 else jnp.bitwise_and(to + 1, 127)
                face = jnp.where(
                    lane == to, pltpu.roll(ref[g * 8 - r0 : g * 8 - r0 + 8], shift, 1), face
                )
        ys[k, d, part] = face

    def take_y(k, d, part, r0, at0, f):
        face = yh[k, d, part]
        end = 128 if d == 0 else 127
        return jnp.concatenate(
            [
                pltpu.roll(face, end - g * 16 - f * half - at0, 1)
                for g in range(r0 // 8, (r0 + CHUNK) // 8)
            ],
            axis=0,
        )

    def put(k, part, at0, z, r0, head, cond, keep_head=True):
        if keep_head:
            hp[k][z + 1, pl.ds(PAD + r0, CHUNK), :] = head
        kp[k][z + 1, pl.ds(PAD + r0, CHUNK), :] = cond
        if r0 == 0:
            xs[k, 0, part, 0, pl.ds(at0, 1), :] = head[0:1]
            xs[k, 0, part, 1, pl.ds(at0, 1), :] = cond[0:1]
        if r0 + CHUNK == rows:
            xs[k, 1, part, 0, pl.ds(at0, 1), :] = head[CHUNK - 1 :]
            xs[k, 1, part, 1, pl.ds(at0, 1), :] = cond[CHUNK - 1 :]
        for d in range(2):
            pack_y(k, d, part, r0, at0, head, cond)

    def remote(src, dst, k, slot, dst_slot, where):
        return pltpu.make_async_remote_copy(
            src_ref=src,
            dst_ref=dst,
            send_sem=h_send.at[k * 12 + slot],
            recv_sem=h_recv.at[k * 12 + dst_slot],
            device_id=where,
            device_id_type=MESH,
        )

    started = []

    def send(copies):
        for copy in copies:
            copy.start()
        started.extend(copies)

    def face_z(k, d):
        to = lax.rem(gz + (n_gz - 1 if d == 0 else 1), n_gz)
        made = []
        for f, ref in enumerate((hp[k], kp[k])):
            src = ref.at[1 if d == 0 else levels, pl.ds(PAD, rows), :]
            dst = ref.at[levels + 1 if d == 0 else 0, pl.ds(PAD, rows), :]
            made.append(remote(src, dst, k, 8 + 2 * f + d, 8 + 2 * f + 1 - d, {"gz": to}))
        return made

    def faces_xy(k, part):
        made = []
        for d in range(2):
            to = lax.rem(gx + (n_gx - 1 if d == 0 else 1), n_gx)
            made.append(
                remote(
                    xs.at[k, d, part],
                    xh.at[k, 1 - d, part],
                    k,
                    2 * part + d,
                    2 * part + 1 - d,
                    {"gx": to},
                )
            )
        for d in range(2):
            to = lax.rem(role + (n_role - 1 if d == 0 else 1), n_role)
            made.append(
                remote(
                    ys.at[k, d, part],
                    yh.at[k, 1 - d, part],
                    k,
                    4 + 2 * part + d,
                    4 + 2 * part + 1 - d,
                    {"role": to},
                )
            )
        return made

    mean_v[:, CAP * rows :, :] = jnp.zeros((layers, 256 - CAP * rows, 2 * cols), jnp.bfloat16)
    for load in loads[3:8]:
        load.wait()

    def start_layer(j):
        for r0 in range(0, rows, CHUNK):
            rs = pl.ds(r0, CHUNK)
            sum_s = None
            sum_h = None
            for i in range(LEVELS_PER_LAYER):
                z = j * LEVELS_PER_LAYER + i
                head = hp[0][z + 1, pl.ds(PAD + r0, CHUNK), :]
                vn = vn_v[z, rs, :]
                la = jnp.log(la_v[z, rs, :]) * LOG2E
                m = 1.0 - 1.0 / vn
                la_v[z, rs, :] = la
                m_v[z, rs, :] = m
                sat, cond = curves(head, la, vn, m, ks_v[z, rs, :])
                th_v[z, rs, :] = po_v[z, rs, :] * sat
                part, at0 = place_of(z)
                put(0, part, at0, z, r0, head, cond, keep_head=False)
                sum_s = sat if sum_s is None else sum_s + sat
                sum_h = head if sum_h is None else sum_h + head
            mean_h = sum_h * 0.25
            lh_v[j, rs, :] = mean_h
            for f, mean in enumerate((mean_h, sum_s * 0.25)):
                for piece, value in enumerate(split3(mean)):
                    mean_v[
                        j,
                        piece * rows + r0 : piece * rows + r0 + CHUNK,
                        f * cols : (f + 1) * cols,
                    ] = value

    start_layer(0)
    start_layer(layers - 1)

    for j in range(1, layers - 1):
        start_layer(j)

    for j in range(layers):
        out = jnp.dot(sel_v[...], mean_v[j], preferred_element_type=jnp.float32)
        tx_v[pl.ds(j, groups * CAP, stride=tile), :] = out[:, :cols]
        tx_v[pl.ds(layers + j, groups * CAP, stride=tile), :] = out[:, cols:]
    rx_v[pl.ds(pl.multiple_of(me * per, 8), per), :] = tx_v[
        pl.ds(pl.multiple_of(me * per, 8), per), :
    ]
    pl.semaphore_wait(barrier, (n_gx - 1) + (n_gz - 1) + 2)

    def tell_line(i, c):
        pl.semaphore_signal(
            line_sem, inc=1, device_id={"gz": lax.rem(gz + i, n_gz)}, device_id_type=MESH
        )
        return c

    lax.fori_loop(1, n_gz, tell_line, 0)

    def zt_copy(i):
        to = lax.rem(gx + i, n_gx)
        return pltpu.make_async_remote_copy(
            src_ref=tp_v.at[to],
            dst_ref=rt_v.at[gx, gz],
            send_sem=zt_send,
            recv_sem=zt_recv,
            device_id={"gx": to},
            device_id_type=MESH,
        )

    def zt_start(i, c):
        zt_copy(i).start()
        return c

    lax.fori_loop(1, n_gx, zt_start, 0)
    rt_v[gx, gz] = tp_v[gx]

    send(face_z(0, 0) + face_z(0, 1))
    for part in range(PARTS):
        send(faces_xy(0, part))


    def land_copy(off_gx, off_gz):
        to_gx = lax.rem(gx + off_gx, n_gx)
        to_gz = lax.rem(gz + off_gz, n_gz)
        to = to_gx * n_gz + to_gz
        pltpu.make_async_remote_copy(
            src_ref=tx_v.at[pl.ds(pl.multiple_of(to * per, 8), per), :],
            dst_ref=rx_v.at[pl.ds(pl.multiple_of(me * per, 8), per), :],
            send_sem=land_send,
            recv_sem=land_recv,
            device_id={"gx": to_gx, "gz": to_gz},
            device_id_type=MESH,
        ).start()

    n_across = n_gx * (n_gz - 1)
    n_land = groups - 1

    def far_first(i):
        step = (i + 1) // 2
        return n_gx // 2 + step * (1 - 2 * lax.rem(i + 1, 2))

    def land_across(i, c):
        land_copy(i // (n_gz - 1), 1 + lax.rem(i, n_gz - 1))
        return c

    def land_along(i, c):
        land_copy(far_first(i - n_across), 0)
        return c

    def land_starts(begin, end):
        if begin < min(end, n_across):
            lax.fori_loop(begin, min(end, n_across), land_across, 0)
        if max(begin, n_across) < end:
            lax.fori_loop(max(begin, n_across), end, land_along, 0)

    at1 = PACE[0] * groups // 64
    at2 = at1 + PACE[1] * groups // 64
    first = n_land - 3 * groups // 64
    land_starts(first, n_land)
    pl.semaphore_wait(line_sem, n_gz - 1)
    land_starts(0, at1)

    def drain(ref, count, sem):
        pltpu.make_async_copy(ref.at[pl.ds(0, count)], ref.at[pl.ds(0, count)], sem).wait()

    drain(tp_v, n_gx - 1, zt_recv)

    def xt_copy(i):
        return pltpu.make_async_remote_copy(
            src_ref=rt_v.at[:, gz],
            dst_ref=rt_v.at[:, gz],
            send_sem=xt_send,
            recv_sem=xt_recv,
            device_id={"gz": lax.rem(gz + i, n_gz)},
            device_id_type=MESH,
        )

    for i in range(1, n_gz):
        xt_copy(i).start()
    land_starts(at1, at2)

    sign = jnp.where(jnp.bitwise_and(lane, 15) < half, 1.0, -1.0)

    def wait_part(k, part):
        views = [(2 * part + d, xh.at[k, d, part]) for d in range(2)]
        views += [(4 + 2 * part + d, yh.at[k, d, part]) for d in range(2)]
        if part == 0:
            for d, plane in enumerate((0, levels + 1)):
                for f, ref in enumerate((hp[k], kp[k])):
                    views.append((8 + 2 * f + d, ref.at[plane, pl.ds(PAD, rows), :]))
        for slot, view in views:
            pltpu.make_async_copy(view, view, h_recv.at[k * 12 + slot]).wait()

        if part == 0:
            for plane, edge, at_end in ((0, 1, 0), (levels + 1, levels, n_gz - 1)):

                @pl.when(gz == at_end)
                def _():
                    hp[k][plane, pl.ds(PAD, rows), :] = hp[k][edge, pl.ds(PAD, rows), :]
                    kp[k][plane, pl.ds(PAD, rows), :] = -kp[k][edge, pl.ds(PAD, rows), :]

        for d in range(2):

            @pl.when(role == (0 if d == 0 else n_role - 1))
            def _():
                yh[k, d, part] = ys[k, d, part] * sign

            @pl.when(gx == (0 if d == 0 else n_gx - 1))
            def _():
                xh[k, d, part, 0] = xs[k, d, part, 0]
                xh[k, d, part, 1] = -xs[k, d, part, 1]

        for d, row in ((0, PAD - 1), (1, PAD + rows)):
            for f, ref in enumerate((hp[k], kp[k])):
                for i in range(half):
                    z = level_at(part, i)
                    ref[z + 1, row : row + 1, :] = xh[k, d, part, f, i : i + 1, :]

    def stencil(k, part, at0, z, r0):
        def cut(ref, plane, shift):
            return ref[k][plane, pl.ds(PAD + r0 + shift, CHUNK), :]

        h, c = cut(hp, z + 1, 0), cut(kp, z + 1, 0)
        first, last = wide_lane == 0, wide_lane == 127
        c_ym = jnp.where(first, take_y(k, 0, part, r0, at0, 1), pltpu.roll(c, 1, 1))
        c_yp = jnp.where(last, take_y(k, 1, part, r0, at0, 1), pltpu.roll(c, 127, 1))
        h_ym = jnp.where(first, take_y(k, 0, part, r0, at0, 0), pltpu.roll(h, 1, 1))
        h_yp = jnp.where(last, take_y(k, 1, part, r0, at0, 0), pltpu.roll(h, 127, 1))
        c_up, c_dn = cut(kp, z, 0), cut(kp, z + 2, 0)
        kf_up = c + c_up
        kf_dn = c + c_dn
        kf_xm = c + cut(kp, z + 1, -1)
        kf_xp = c + cut(kp, z + 1, 1)
        kf_ym = c + c_ym
        kf_yp = c + c_yp
        flux = kf_up * (h - cut(hp, z, 0)) + kf_dn * (h - cut(hp, z + 2, 0))
        flux = flux + kf_xm * (h - cut(hp, z + 1, -1)) + kf_xp * (h - cut(hp, z + 1, 1))
        flux = flux + kf_ym * (h - h_ym) + kf_yp * (h - h_yp)
        diag = 2.0 + ((kf_up + kf_dn) + (kf_xm + kf_xp) + (kf_ym + kf_yp))
        return h, flux + (c_dn - c_up), diag

    def first_half(part, level, i, c):
        z = level(i)
        for r0 in range(0, rows, CHUNK):
            _, resid, diag = stencil(0, part, i, z, r0)
            ra_v[z, pl.ds(r0, CHUNK), :] = resid
            da_v[z, pl.ds(r0, CHUNK), :] = OMEGAS[0] / diag
        return c

    for part in range(PARTS):
        wait_part(0, part)
        for begin, end, level in segments[part]:
            lax.fori_loop(begin, end, functools.partial(first_half, part, level), 0, unroll=2)

    ref3 = rt_v.at[:, pl.ds(0, n_gz - 1)]
    pltpu.make_async_copy(ref3, ref3, xt_recv).wait()

    pieces = jnp.concatenate(split3(rt_v[...].reshape(groups * 8, cols)), axis=1)
    got = jnp.dot(get_v[...], pieces, preferred_element_type=jnp.float32)
    got = got[:, :cols] + got[:, cols : 2 * cols] + got[:, 2 * cols :]
    tq_v[...] = got[:rows]
    rq_v[...] = got[rows:] + (1.0 - act_v[...])

    def root_weight(depth, roots):
        return jnp.where(depth < roots, math.exp(-depth / 4.0), 0.0)

    for r0 in range(0, rows, CHUNK):
        rs = pl.ds(r0, CHUNK)
        roots = rq_v[rs, :]
        total = root_weight(0, roots)
        for depth in range(1, layers * n_gz):
            total = total + root_weight(depth, roots)
        scale = tq_v[rs, :]
        for j in range(layers):
            depth = (gz * layers + j).astype(jnp.float32)
            weight = jnp.where(
                depth < roots, jnp.exp(jnp.full((CHUNK, 128), -0.25, jnp.float32) * depth), 0.0
            )
            lh = lh_v[j, rs, :]
            stress = 1.0 / (1.0 + lh * lh * (1.0 / 2.25))
            sk_v[j, rs, :] = 2.0 * (scale * (weight / total) * stress)

    def curve_into(k, part, at0, z, r0, head):
        rs = pl.ds(r0, CHUNK)
        sat, cond = curves(head, la_v[z, rs, :], vn_v[z, rs, :], m_v[z, rs, :], ks_v[z, rs, :])
        put(k, part, at0, z, r0, head, cond)
        gain = po_v[z, rs, :] * sat - th_v[z, rs, :]
        ra_v[z, rs, :] = (gain + gain) + sk_v[z // LEVELS_PER_LAYER, rs, :]

    def second_half(part, level, i, c):
        z = level(i)
        for r0 in range(0, rows, CHUNK):
            rs = pl.ds(r0, CHUNK)
            resid = ra_v[z, rs, :] + sk_v[z // LEVELS_PER_LAYER, rs, :]
            head = hp[0][z + 1, pl.ds(PAD + r0, CHUNK), :]
            curve_into(1, part, i, z, r0, head - resid * da_v[z, rs, :])
        return c

    def sweep_level(k, part, level, i, c):
        z = level(i)
        for r0 in range(0, rows, CHUNK):
            rs = pl.ds(r0, CHUNK)
            head, flux, diag = stencil(k, part, i, z, r0)
            head = head - (ra_v[z, rs, :] + flux) * (OMEGAS[k] / diag)
            if k + 1 < SWEEPS:
                curve_into(k + 1, part, i, z, r0, head)
            else:
                out_p[z, rs, :] = head
        return c

    def run(k, part, body):
        for begin, end, level in segments[part]:
            lax.fori_loop(begin, end, functools.partial(body, part, level), 0, unroll=2)
            if k < SWEEPS and part == 0 and begin == 0:
                send(face_z(k, 0) + face_z(k, 1))
        if k < SWEEPS:
            send(faces_xy(k, part))

    for part in range(PARTS):
        run(1, part, second_half)
    land_starts(at2, first)
    for part in range(PARTS):
        wait_part(1, part)
        run(2, part, functools.partial(sweep_level, 1))

    for load in loads[8:]:
        load.wait()
    all_but_me = rx_v.at[pl.ds(0, (groups - 1) * per), :]
    pltpu.make_async_copy(all_but_me, all_but_me, land_recv).wait()
    sub = min(8, n_gx)
    n_layers = layers * n_gz
    for block in range(n_gx // sub):
        for r in range(CAP):
            b0 = block * sub

            def slots(ref, at3, stride):
                return ref[pl.ds(at3, sub, stride=stride), :]

            tpot = slots(tr_v, b0 * CAP + r, CAP)
            air = slots(ai_v, b0 * CAP + r, CAP)
            roots = slots(ro_v, b0 * CAP + r, CAP).astype(jnp.float32)
            weights = [root_weight(d, roots) for d in range(n_layers)]
            total = weights[0]
            for weight in weights[1:]:
                total = total + weight
            temps, kappa, upt = [], [], []
            for d in range(n_layers):
                bz, j = d // layers, d % layers
                base = (b0 * n_gz + bz) * per + r * tile + j
                lh = slots(rx_v, base, n_gz * per)
                ls = slots(rx_v, base + layers, n_gz * per)
                stress = 1.0 / (1.0 + lh * lh * (1.0 / 2.25))
                upt.append(0.3 * (tpot * (weights[d] / total) * stress))
                kappa.append(0.25 + 0.9 * ls)
                temps.append(slots(lt_v, (b0 * CAP + r) * n_layers + d, CAP * n_layers))
            mids = [0.5 * (kappa[d] + kappa[d + 1]) for d in range(n_layers - 1)]
            old = temps
            for _ in range(HEAT_STEPS):
                fresh = []
                for d in range(n_layers):
                    move = (
                        kappa[0] * (air - temps[0])
                        if d == 0
                        else mids[d - 1] * (temps[d - 1] - temps[d])
                    )
                    if d < n_layers - 1:
                        move = move + mids[d] * (temps[d + 1] - temps[d])
                    fresh.append(temps[d] + 0.2 * move - upt[d])
                temps = fresh
            filled = cnt_v[b0 : b0 + sub, :] > r
            for d in range(n_layers):
                out_lt[pl.ds((b0 * CAP + r) * n_layers + d, sub, stride=CAP * n_layers), :] = (
                    jnp.where(filled, temps[d], old[d])
                )

    for part in range(PARTS):
        wait_part(2, part)
        run(3, part, functools.partial(sweep_level, 2))

    for copy in started:
        copy.wait_send()
    drain(tp_v, n_gx - 1, zt_send)
    pltpu.make_async_copy(ref3, ref3, xt_send).wait()
    pltpu.make_async_copy(all_but_me, all_but_me, land_send).wait()


def solution(mesh):
    n_role, n_gx, n_gz = (mesh.shape[a] for a in ("role", "gx", "gz"))

    def local(p, al, vn, ks, po, owner, land, transp, air, roots):
        levels, rows, cols = p.shape
        layers = levels // LEVELS_PER_LAYER
        n_layers = layers * n_gz
        groups = n_gx * n_gz
        slots = n_gx * CAP
        f32 = jnp.float32
        cell = pltpu.VMEM((levels, rows, cols), f32)
        padded = pltpu.VMEM((levels + 2, rows + 2 * PAD, cols), f32)
        xface = pltpu.VMEM((SWEEPS, 2, PARTS, 2, levels // PARTS, cols), f32)
        yface = pltpu.VMEM((SWEEPS, 2, PARTS, 8, cols), f32)
        line = pltpu.VMEM((slots, cols), f32)
        payload = pltpu.VMEM((groups * CAP * 2 * layers, cols), f32)
        dma = pltpu.SemaphoreType.DMA
        head, temps = pl.pallas_call(
            functools.partial(kernel, n_role, n_gx, n_gz),
            out_shape=(
                jax.ShapeDtypeStruct(p.shape, f32),
                jax.ShapeDtypeStruct((slots * n_layers, cols), f32),
            ),
            in_specs=[pl.BlockSpec(memory_space=pltpu.HBM)] * 10,
            out_specs=[pl.BlockSpec(memory_space=pltpu.VMEM)] * 2,
            scratch_shapes=[
                cell,
                cell,
                cell,
                cell,
                cell,
                cell,
                cell,
                cell,
                padded,
                padded,
                padded,
                padded,
                padded,
                padded,
                xface,
                xface,
                yface,
                yface,
                pltpu.VMEM(owner.shape[::-1], jnp.int32),
                pltpu.VMEM((slots * n_layers, cols), f32),
                line,
                line,
                pltpu.VMEM((slots, cols), jnp.int32),
                pltpu.VMEM((groups * CAP, 256), jnp.bfloat16),
                pltpu.VMEM((2 * rows, groups * 8), jnp.bfloat16),
                pltpu.VMEM((rows, cols), f32),
                pltpu.VMEM((n_gx, cols), f32),
                pltpu.VMEM((n_gx, 8, cols), f32),
                pltpu.VMEM((n_gx, n_gz, 8, cols), f32),
                pltpu.VMEM((rows, cols), f32),
                pltpu.VMEM((rows, cols), f32),
                pltpu.VMEM((layers, rows, cols), f32),
                pltpu.VMEM((layers, rows, cols), f32),
                pltpu.VMEM((layers, 256, 2 * cols), jnp.bfloat16),
                payload,
                payload,
                dma((10,)),
                dma,
                dma,
                dma,
                dma,
                dma((SWEEPS * 12,)),
                dma((SWEEPS * 12,)),
                dma,
                dma,
                pltpu.SemaphoreType.REGULAR,
            ],
            compiler_params=pltpu.CompilerParams(
                collective_id=0, has_side_effects=True, vmem_limit_bytes=28 * 1024 * 1024
            ),
        )(
            *[
                pltpu.with_memory_space_constraint(x, pltpu.HBM)
                for x in (
                    p,
                    al,
                    vn,
                    ks,
                    po,
                    owner.T,
                    land.reshape(slots * n_layers, cols),
                    transp.reshape(slots, cols),
                    air.reshape(slots, cols),
                    roots.reshape(slots, cols),
                )
            ]
        )
        return head, temps.reshape(land.shape)

    grid = P("gz", "gx", "role")
    slot = P("role", ("gx", "gz"), None, None)
    return jax.shard_map(
        local,
        mesh=mesh,
        in_specs=(grid,) * 5 + (P(), P("role", ("gx", "gz"), None, None, None)) + (slot,) * 3,
        out_specs=(grid, P("role", ("gx", "gz"), None, None, None)),
        check_vma=False,
    )
```
